256 devices in a mesh: dp: 16 (over z, core), frame: 16 (over x, y).
Axes of the slice: x: 4, y: 4, z: 8, core: 2. Of those that a mesh axis runs over, the one named last changes fastest.
Arguments:
- latents: bfloat16 [16, 32, 128, 1280], P('dp', 'frame'), may hold values from -330 to 330
- timestep: int32 [16], P('dp'), may hold values from 0 to 999
- norm_gain: float32 [1280], replicated, may hold values from 0.1 to 1.9
- time_weight: bfloat16 [320, 1280], P('dp'), may hold values from -0.3125 to 0.3125
- conv_weight: bfloat16 [3, 1280, 1280], P(None, ('dp', 'frame')), may hold values from -0.09375 to 0.09375
- attend_weight: bfloat16 [1280, 3840], P(('dp', 'frame')), may hold values from -0.3354102 to 0.3354102
- output_weight: bfloat16 [1280, 1280], P(('dp', 'frame')), may hold values from -0.15625 to 0.15625
Outputs:
- block_out: bfloat16 [16, 32, 128, 1280], P('dp', 'frame')
The draws below stay inside these ranges and needn't reach their ends.
All inputs are finite; a program needn't handle non-finite values.
Results may differ from the reference program's by a relative error of at most 0.0051.
Values may be sent and summed in bfloat16 or wider, within the bound.
No kernel may reach another device: no remote copies, remote signals or barrier semaphores. Data moves between devices by JAX's collectives and lax.ppermute only.
A program may use at most 128 MiB of HBM per device.

```python
import math
import jax
import jax.numpy as jnp
from jax import lax

C = 1280
HEADS = 20
HD = 64
GROUPS = 32
TEMB = 320
PIX = 128
FRAMES = 32
CLIPS = 16


def draw_latents(key, part):
    key_base, key_pixel, key_chan, key_frame = jax.random.split(key, 4)
    shape = (CLIPS, FRAMES, PIX, C)
    ladder = jnp.arange(FRAMES, dtype=jnp.float32)
    frame_ladder = 3.0 ** (ladder / max(FRAMES - 1, 1))
    frame_factor = jnp.exp(jax.random.uniform(key_frame, (CLIPS, FRAMES, 1, 1), jnp.float32, math.log(0.5), math.log(2.0)))
    frame_scale = frame_ladder[None, :, None, None] * frame_factor
    pixel_scale = jnp.exp(jax.random.uniform(key_pixel, (CLIPS, 1, PIX, 1), jnp.float32, math.log(0.3), math.log(3.0)))
    chan_scale = jnp.exp(jax.random.uniform(key_chan, (1, 1, 1, C), jnp.float32, math.log(0.3), math.log(3.0)))
    base = jnp.clip(jax.random.normal(key_base, shape, jnp.float32), -6.0, 6.0)
    values = base * frame_scale * pixel_scale * chan_scale
    return values.astype(jnp.bfloat16)


def draw_attend_weight(key, part):
    key_query = jax.random.fold_in(key, 0)
    scale = 1.0 / math.sqrt(C)
    values = jnp.clip(jax.random.normal(key_query, (C, 3 * C), jnp.float32), -6.0, 6.0) * scale
    return values.astype(jnp.bfloat16)


def place_ends(array, stream_key, low, largest):
    longest = array.shape.index(max(array.shape))
    spots = []
    for shift in (0, 1):
        where = [jax.random.randint(jax.random.fold_in(stream_key, axis), (), 0, length) for axis, length in enumerate(array.shape)]
        where[longest] = (where[longest] + shift) % array.shape[longest]
        spots.append(tuple(where))
    return array.at[spots[0]].set(low).at[spots[1]].set(largest)


def block_levels(key, extent, cuts, least, top_value):
    def one(dim, blocks):
        heights = jax.random.uniform(jax.random.fold_in(jax.random.fold_in(key, 6), dim), (blocks,), jnp.float32, least / len(cuts), top_value / len(cuts))
        return jnp.repeat(jnp.exp(heights), extent[dim] // blocks).reshape((-1,) + (1,) * (len(extent) - dim - 1))

    gain = one(*cuts[0])
    for cut in cuts[1:]:
        gain = gain * one(*cut)
    return gain


def scatter_about(rng, extent, width, limit, cuts=(), held_as=jnp.bfloat16):
    entries = jax.random.normal(rng, extent, jnp.float32) * width
    if len(cuts) > 0:
        entries = block_levels(rng, extent, cuts, -0.22, 0.18) * entries
    return jnp.clip(entries, min=-limit, max=limit).astype(held_as)


def setup_inputs(seed: int = 0) -> dict:
    key_of = jax.random.split(jax.random.key(seed), 8)
    return {
        "latents": draw_latents(jax.random.fold_in(key_of[7], 71), 0),
        "timestep": place_ends(jax.random.randint(key_of[1], (CLIPS,), 0, 1000), jax.random.fold_in(key_of[1], 1), 0, 999).astype(jnp.int32),
        "norm_gain": jnp.clip(1.0 + 0.18 * jax.random.normal(key_of[2], (C,), jnp.float32), 0.1, 1.9),
        "time_weight": scatter_about(key_of[3], (TEMB, C), TEMB ** -0.5, 0.3125, ((0, 16),)),
        "conv_weight": scatter_about(key_of[4], (3, C, C), (3 * C) ** -0.5, 0.09375, ((1, 256),)),
        "attend_weight": draw_attend_weight(jax.random.fold_in(key_of[7], 71), 0),
        "output_weight": scatter_about(key_of[6], (C, C), C ** -0.5, 0.15625, ((0, 256),)),
    }


def sinusoid(timestep):
    half_dim = TEMB // 2
    ladder = jnp.arange(half_dim, dtype=jnp.float32)
    freqs = jnp.exp(-math.log(10000.0) * ladder / half_dim)
    angles = timestep.astype(jnp.float32)[:, None] * freqs[None, :]
    return jnp.concatenate([jnp.cos(angles), jnp.sin(angles)], axis=-1)

def reference(latents, timestep, norm_gain, time_weight, conv_weight, attend_weight, output_weight):
    features = sinusoid(timestep).astype(jnp.bfloat16)
    time_bias = jnp.dot(features, time_weight, preferred_element_type=jnp.float32)

    def one_clip(packed):
        clip, bias_row = packed
        values = clip.astype(jnp.float32)
        grouped = values.reshape(FRAMES, PIX, GROUPS, C // GROUPS)
        center = lax.optimization_barrier(jnp.mean(grouped, axis=(0, 1, 3)))
        spread = lax.optimization_barrier(jnp.mean((grouped - center[None, None, :, None]) ** 2, axis=(0, 1, 3)))
        normed_group = (grouped - center[None, None, :, None]) / jnp.sqrt(spread[None, None, :, None] + 1e-05)
        scaled = normed_group.reshape(FRAMES, PIX, C) * norm_gain
        hidden = jax.nn.silu(scaled).astype(jnp.bfloat16)
        padded = jnp.pad(hidden, ((1, 1), (0, 0), (0, 0)))
        conv = jnp.zeros((FRAMES * PIX, C), jnp.float32)
        for offset in range(3):
            window = padded[offset:offset + FRAMES].reshape(FRAMES * PIX, C)
            conv = conv + jnp.dot(window, conv_weight[offset], preferred_element_type=jnp.float32)
        conv = conv + bias_row[None, :]
        residual = (values.reshape(FRAMES * PIX, C) + conv).astype(jnp.bfloat16)
        rows = residual.astype(jnp.float32)
        row_mean = lax.optimization_barrier(jnp.mean(rows, axis=-1, keepdims=True))
        row_var = lax.optimization_barrier(jnp.mean((rows - row_mean) ** 2, axis=-1, keepdims=True))
        normed = ((rows - row_mean) / jnp.sqrt(row_var + 1e-05)).astype(jnp.bfloat16)
        triple = jnp.dot(normed, attend_weight, preferred_element_type=jnp.float32).astype(jnp.bfloat16)
        triple = triple.astype(jnp.float32).reshape(FRAMES, PIX, 3, HEADS, HD)
        queries = triple[:, :, 0]
        key_part = triple[:, :, 1]
        value_part = triple[:, :, 2]
        scores = jnp.einsum('fphd,gphd->phfg', queries, key_part) / math.sqrt(HD)
        peak = lax.optimization_barrier(jnp.max(scores, axis=-1, keepdims=True))
        expo = jnp.exp(scores - peak)
        probs = (expo / lax.optimization_barrier(jnp.sum(expo, axis=-1, keepdims=True))).astype(jnp.bfloat16)
        attended = jnp.einsum('phfg,gphd->fphd', probs.astype(jnp.float32), value_part)
        attended = attended.astype(jnp.bfloat16).reshape(FRAMES * PIX, C)
        mixed = rows + jnp.dot(attended, output_weight, preferred_element_type=jnp.float32)
        return mixed.astype(jnp.bfloat16).reshape(FRAMES, PIX, C)
    return lax.map(one_clip, (latents, time_bias))
```

```python
import math

import jax
import jax.numpy as jnp
from jax import lax
from jax.experimental import pallas as pl
from jax.experimental.pallas import tpu as pltpu
from jax.sharding import Mesh
from jax.sharding import PartitionSpec as P


HEADS = 20
HD = 64
GROUPS = 32
TEMB = 320
FRAME = ("x", "y")
DP = ("z", "core")
ALL = ("z", "core", "x", "y")


def shifted(array, axis, step):
    count = lax.axis_size(axis)
    return lax.ppermute(array, axis, [(i, (i + step) % count) for i in range(count)])


def small_ring(piece, axis):
    back = shifted(piece, axis, 1)
    ahead = shifted(piece, axis, -1)
    return [piece, back, ahead, shifted(back, axis, 1)]


def halved_ring(piece, axis, reach):
    pieces = [piece]
    back = ahead = piece
    for _ in range(reach - 1):
        back = shifted(back, axis, 1)
        ahead = shifted(ahead, axis, -1)
        pieces += [back, ahead]
    half = piece.shape[0] // 2
    far = jnp.concatenate(
        [shifted(back[:half], axis, 1), shifted(ahead[half:], axis, -1)], axis=0
    )
    return pieces + [far]


def ring_offsets(reach):
    places = [0]
    for step in range(1, reach):
        places += [-step, step]
    return places + [reach]


def digits(index, sizes):
    out = []
    for size in reversed(sizes):
        out.append(index % size)
        index = index // size
    return out[::-1]


def looked_up(index, table):
    value = jnp.zeros_like(index)
    for place, entry in enumerate(table):
        value = jnp.where(index == place, entry, value)
    return value


def selection(channel):
    source = lax.broadcasted_iota(jnp.int32, (channel.shape[0], channel.shape[0]), 0)
    return (source == channel[None, :]).astype(jnp.bfloat16)


def channel_of(z, core, x, y, row):
    return z * 160 + core * 80 + x * 20 + y * 5 + row


def moved(array, table):
    return jnp.dot(array, table, preferred_element_type=jnp.float32).astype(jnp.bfloat16)


def in_order(pieces, axis, offsets):
    count = lax.axis_size(axis)
    spots = (lax.axis_index(axis) + jnp.asarray(offsets, jnp.int32)) % count
    pick = (jnp.arange(count)[:, None] == spots[None, :]).astype(jnp.float32)
    stacked = jnp.stack(pieces)
    return jnp.sum(pick.reshape(count, count, *(1,) * (stacked.ndim - 1)) * stacked[None], axis=1)


def sinusoid(timestep):
    half_dim = TEMB // 2
    ladder = jnp.arange(half_dim, dtype=jnp.float32)
    freqs = jnp.exp(-math.log(10000.0) * ladder / half_dim)
    angles = timestep.astype(jnp.float32)[:, None] * freqs[None, :]
    return jnp.concatenate([jnp.cos(angles), jnp.sin(angles)], axis=-1)


def attend_kernel(query_ref, key_ref, value_ref, out_ref):
    query, key, value = query_ref[...], key_ref[...], value_ref[...]
    count = query.shape[0]
    first = lax.broadcasted_iota(jnp.int32, query.shape, 1) < HD
    same = (
        lax.broadcasted_iota(jnp.int32, (count, count), 0) % 8
        == lax.broadcasted_iota(jnp.int32, (count, count), 1) % 8
    )
    results = []
    for mine in (first, jnp.logical_not(first)):
        part = jnp.where(mine, query, jnp.zeros_like(query))
        scores = lax.dot_general(
            part, key, (((1,), (1,)), ((), ())), preferred_element_type=jnp.float32
        ) * (1.0 / math.sqrt(HD))
        scores = jnp.where(same, scores, -3e38)
        peak = jnp.max(scores, axis=-1, keepdims=True)
        expo = jnp.exp(scores - peak)
        probs = (expo / jnp.sum(expo, axis=-1, keepdims=True)).astype(jnp.bfloat16)
        results.append(jnp.dot(probs, value, preferred_element_type=jnp.float32))
    out_ref[...] = jnp.where(first, results[0], results[1]).astype(jnp.bfloat16)


def attend(triple):
    rows, width = triple.shape
    channels = width // 3
    pairs = channels // 128
    block = lambda shift: pl.BlockSpec((rows, 128), lambda i: (0, i + shift))
    return pl.pallas_call(
        attend_kernel,
        grid=(pairs,),
        in_specs=[block(0), block(pairs), block(2 * pairs)],
        out_specs=block(0),
        out_shape=jax.ShapeDtypeStruct((rows, channels), jnp.bfloat16),
        cost_estimate=pl.CostEstimate(
            flops=4 * rows * rows * 128 * 2 * pairs,
            bytes_accessed=4 * rows * channels * 2,
            transcendentals=rows * rows * HEADS,
        ),
    )(triple, triple, triple)


def shards(latents, timestep, norm_gain, time_weight, conv_weight, attend_weight, output_weight):
    _, frames_dev, pixels, channels = latents.shape
    half = channels // 2
    my = {axis: lax.axis_index(axis) for axis in ALL}
    frame = my["x"] * 4 + my["y"]

    time_slice = lax.dynamic_index_in_dim(time_weight.reshape(20, 16, 80), frame, 1, False)
    colors = []
    for side in range(2):
        cut = slice(side * half, (side + 1) * half)
        colors += [conv_weight[t, :, cut] for t in range(3)] + [output_weight[:, cut]]
    piece = jnp.concatenate(colors + [time_slice.reshape(5, 320)], axis=1)
    stage = lax.all_gather(piece, "z", axis=0)
    columns = 4 * half

    def along(piece_list):
        return jnp.concatenate(piece_list, axis=0)

    color_parts = []
    for side, (inner, outer) in enumerate((("x", "y"), ("y", "x"))):
        chunk = stage[:, :, side * columns : (side + 1) * columns].reshape(40, columns)
        chunk = along(small_ring(chunk, inner))
        pieces = halved_ring(chunk, outer, 2)
        near, far = along(pieces[:3]), pieces[3]
        other = [shifted(near, "core", 1), shifted(far, "core", 1)]
        color_parts.append(along([near, far] + other))

    square = along([p[None] for p in small_ring(attend_weight, "x")])
    square = along(small_ring(square, "y")).reshape(80, 3 * channels)
    pieces = halved_ring(square, "z", 4)
    groups = [along(pieces[:3]), along(pieces[3:5]), along(pieces[5:7]), pieces[7]]
    attend_full = along(groups + [shifted(group, "core", 1) for group in groups])

    values = lax.all_to_all(latents, FRAME, split_axis=2, concat_axis=1, tiled=True)
    values = values.reshape(-1, channels).astype(jnp.float32)

    here = latents.reshape(-1, channels).astype(jnp.float32)
    width = channels // GROUPS
    members = here.shape[0] * width
    mean_here = jnp.sum(jnp.sum(here, axis=0).reshape(GROUPS, width), axis=1) / members
    deviate = here - jnp.repeat(mean_here, width)[None, :]
    square_here = jnp.sum(jnp.sum(deviate * deviate, axis=0).reshape(GROUPS, width), axis=1)
    features = sinusoid(timestep).astype(jnp.bfloat16).reshape(8, 2, 20)
    time_rows = stage[:, :, 2 * columns :].reshape(160, 80)
    time_other = shifted(time_rows, "core", 1)
    bias_here = jnp.zeros((1, 80), jnp.float32)
    for core, rows in ((my["core"], time_rows), (1 - my["core"], time_other)):
        part = lax.dynamic_index_in_dim(features, core, 1, False).reshape(1, 160)
        bias_here = bias_here + jnp.dot(part, rows, preferred_element_type=jnp.float32)
    sums = jnp.concatenate([mean_here, square_here, bias_here[0]])[None, :]
    shifts = [0, -1, -2, -3]
    sums = in_order([sums] + [shifted(sums, "y", s) for s in (1, 2, 3)], "y", shifts)
    sums = in_order([sums] + [shifted(sums, "x", s) for s in (1, 2, 3)], "x", shifts)
    sums = sums.reshape(16, -1)
    means, squares = sums[:, :GROUPS], sums[:, GROUPS : 2 * GROUPS]
    time_bias = sums[:, 2 * GROUPS :].reshape(1, channels)
    center = jnp.mean(means, axis=0)
    spread = jnp.sum(squares, axis=0) + members * jnp.sum((means - center) ** 2, axis=0)
    spread = spread / (16 * members)
    scale = norm_gain / jnp.sqrt(jnp.repeat(spread, width) + 1e-05)
    scaled = (values - jnp.repeat(center, width)[None, :]) * scale[None, :]
    hidden = jax.nn.silu(scaled).astype(jnp.bfloat16)

    spot = jnp.arange(channels, dtype=jnp.int32)
    two, four = ring_offsets(2), ring_offsets(4)
    tables = []
    for side in range(2):
        part, outer, inner, z, row = digits(spot, (2, 4, 4, 8, 5))
        core = jnp.where(part == 0, my["core"], 1 - my["core"])
        outer, inner = looked_up(outer, two), looked_up(inner, [0, -1, 1, -2])
        x, y = (inner, outer) if side == 0 else (outer, inner)
        tables.append(
            selection(channel_of(z, core, (my["x"] + x) % 4, (my["y"] + y) % 4, row))
        )
    part, z, y, x, row = digits(spot, (2, 8, 4, 4, 5))
    core = jnp.where(part == 0, my["core"], 1 - my["core"])
    z = (my["z"] + looked_up(z, four)) % 8
    x = (my["x"] + looked_up(x, [0, -1, 1, -2])) % 4
    y = (my["y"] + looked_up(y, [0, -1, 1, -2])) % 4
    attend_table = selection(channel_of(z, core, x, y, row))

    conv = []
    for side in range(2):
        product = jnp.dot(
            moved(hidden, tables[side]),
            color_parts[side][:, : 3 * half],
            preferred_element_type=jnp.float32,
        )
        taps = [product[:, t * half : (t + 1) * half] for t in range(3)]
        edge = jnp.zeros((8, half), jnp.float32)
        before = jnp.concatenate([edge, taps[0][:-8]], axis=0)
        after = jnp.concatenate([taps[2][8:], edge], axis=0)
        conv.append(before + taps[1] + after)
    conv = jnp.concatenate(conv, axis=1) + time_bias
    residual = (values + conv).astype(jnp.bfloat16)
    rows = residual.astype(jnp.float32)
    row_mean = jnp.mean(rows, axis=-1, keepdims=True)
    row_var = jnp.mean((rows - row_mean) ** 2, axis=-1, keepdims=True)
    normed = ((rows - row_mean) / jnp.sqrt(row_var + 1e-05)).astype(jnp.bfloat16)
    triple = jnp.dot(
        moved(normed, attend_table), attend_full, preferred_element_type=jnp.float32
    ).astype(jnp.bfloat16)
    attended = attend(triple)
    projected = [
        jnp.dot(
            moved(attended, tables[side]),
            color_parts[side][:, 3 * half :],
            preferred_element_type=jnp.float32,
        )
        for side in range(2)
    ]
    mixed = (rows + jnp.concatenate(projected, axis=1)).astype(jnp.bfloat16)
    mixed = mixed.reshape(1, -1, 8, channels)
    return lax.all_to_all(mixed, FRAME, split_axis=1, concat_axis=2, tiled=True)


def solution(mesh):
    split = Mesh(mesh.devices.reshape(8, 2, 4, 4), ALL)
    placed = (
        P(DP, FRAME, None, None),
        P(DP),
        P(),
        P(DP, None),
        P(None, ALL, None),
        P(ALL, None),
        P(ALL, None),
    )
    return jax.shard_map(
        shards, mesh=split, in_specs=placed, out_specs=P(DP, FRAME, None, None), check_vma=False
    )
```

```python
import math

import jax
import jax.numpy as jnp
from jax import lax
from jax.experimental import pallas as pl
from jax.experimental.pallas import tpu as pltpu
from jax.sharding import Mesh
from jax.sharding import PartitionSpec as P


HEADS = 20
HD = 64
GROUPS = 32
TEMB = 320
FRAME = ("x", "y")
DP = ("z", "core")
ALL = ("z", "core", "x", "y")


def shifted(array, axis, step):
    count = lax.axis_size(axis)
    return lax.ppermute(array, axis, [(i, (i + step) % count) for i in range(count)])


def small_ring(piece, axis):
    back = shifted(piece, axis, 1)
    ahead = shifted(piece, axis, -1)
    return [piece, back, ahead, shifted(back, axis, 1)]


def halved_ring(piece, axis, reach):
    pieces = [piece]
    back = ahead = piece
    for _ in range(reach - 1):
        back = shifted(back, axis, 1)
        ahead = shifted(ahead, axis, -1)
        pieces += [back, ahead]
    half = piece.shape[0] // 2
    far = jnp.concatenate(
        [shifted(back[:half], axis, 1), shifted(ahead[half:], axis, -1)], axis=0
    )
    return pieces + [far]


def ring_offsets(reach):
    places = [0]
    for step in range(1, reach):
        places += [-step, step]
    return places + [reach]


def digits(index, sizes):
    out = []
    for size in reversed(sizes):
        out.append(index % size)
        index = index // size
    return out[::-1]


def looked_up(index, table):
    value = jnp.zeros_like(index)
    for place, entry in enumerate(table):
        value = jnp.where(index == place, entry, value)
    return value


def selection(channel):
    source = lax.broadcasted_iota(jnp.int32, (2 * GROUPS * 20, channel.shape[0]), 0)
    return (source == channel[None, :]).astype(jnp.bfloat16)


def channel_of(z, core, x, y, row):
    return z * 160 + core * 80 + x * 20 + y * 5 + row


def moved(array, table):
    return jnp.dot(array, table, preferred_element_type=jnp.float32).astype(jnp.bfloat16)


def in_order(pieces, axis, offsets):
    count = lax.axis_size(axis)
    spots = (lax.axis_index(axis) + jnp.asarray(offsets, jnp.int32)) % count
    pick = (jnp.arange(count)[:, None] == spots[None, :]).astype(jnp.float32)
    stacked = jnp.stack(pieces)
    return jnp.sum(pick.reshape(count, count, *(1,) * (stacked.ndim - 1)) * stacked[None], axis=1)


def sinusoid(timestep):
    half_dim = TEMB // 2
    ladder = jnp.arange(half_dim, dtype=jnp.float32)
    freqs = jnp.exp(-math.log(10000.0) * ladder / half_dim)
    angles = timestep.astype(jnp.float32)[:, None] * freqs[None, :]
    return jnp.concatenate([jnp.cos(angles), jnp.sin(angles)], axis=-1)


def attend_kernel(rows_ref, table_ref, query_ref, key_ref, value_ref, out_ref, held_ref):
    count = rows_ref.shape[0]
    frames = count // 8

    @pl.when(pl.program_id(0) == 0)
    def _():
        to = lax.broadcasted_iota(jnp.int32, (count, count), 0)
        source = lax.broadcasted_iota(jnp.int32, (count, count), 1)
        by_pixel = (source == (to % frames) * 8 + to // frames).astype(jnp.bfloat16)
        held_ref[...] = moved(by_pixel, moved(rows_ref[...], table_ref[...]))

    held = held_ref[...]
    query, key, value = [
        jnp.dot(held, ref[...], preferred_element_type=jnp.float32).astype(jnp.bfloat16)
        for ref in (query_ref, key_ref, value_ref)
    ]
    group = count // 2
    first = lax.broadcasted_iota(jnp.int32, (group, 128), 1) < HD
    same = (
        lax.broadcasted_iota(jnp.int32, (group, group), 0) // frames
        == lax.broadcasted_iota(jnp.int32, (group, group), 1) // frames
    )
    for place in range(2):
        cut = slice(place * group, (place + 1) * group)
        results = []
        for mine in (first, jnp.logical_not(first)):
            part = jnp.where(mine, query[cut], jnp.zeros_like(query[cut]))
            scores = lax.dot_general(
                part, key[cut], (((1,), (1,)), ((), ())), preferred_element_type=jnp.float32
            ) * (1.0 / math.sqrt(HD))
            scores = jnp.where(same, scores, -3e38)
            peak = jnp.max(scores, axis=-1, keepdims=True)
            expo = jnp.exp(scores - peak)
            probs = (expo / jnp.sum(expo, axis=-1, keepdims=True)).astype(jnp.bfloat16)
            results.append(jnp.dot(probs, value[cut], preferred_element_type=jnp.float32))
        out_ref[cut, :] = jnp.where(first, results[0], results[1]).astype(jnp.bfloat16)


def attend(normed, table, weights):
    count, channels = normed.shape
    pairs = channels // 128
    whole = lambda array: pl.BlockSpec(array.shape, lambda i: (0, 0))
    block = lambda shift: pl.BlockSpec((channels, 128), lambda i: (0, i + shift))
    return pl.pallas_call(
        attend_kernel,
        grid=(pairs,),
        in_specs=[whole(normed), whole(table), block(0), block(pairs), block(2 * pairs)],
        out_specs=pl.BlockSpec((count, 128), lambda i: (0, i)),
        out_shape=jax.ShapeDtypeStruct((count, channels), jnp.bfloat16),
        scratch_shapes=[pltpu.VMEM((count, channels), jnp.bfloat16)],
        cost_estimate=pl.CostEstimate(
            flops=2 * count * channels * 4 * channels,
            bytes_accessed=8 * channels * channels + 4 * count * channels,
            transcendentals=count * count * HEADS // 2,
        ),
    )(normed, table, weights, weights, weights)


def project_kernel(attended_ref, table_ref, rows_ref, weight_ref, out_ref, held_ref):
    count = rows_ref.shape[0]
    frames = count // 8

    @pl.when(pl.program_id(0) == 0)
    def _():
        to = lax.broadcasted_iota(jnp.int32, (count, count), 0)
        source = lax.broadcasted_iota(jnp.int32, (count, count), 1)
        by_frame = (source == (to % 8) * frames + to // 8).astype(jnp.bfloat16)
        held_ref[...] = moved(by_frame, moved(attended_ref[...], table_ref[...]))

    product = jnp.dot(held_ref[...], weight_ref[...], preferred_element_type=jnp.float32)
    out_ref[...] = (rows_ref[...].astype(jnp.float32) + product).astype(jnp.bfloat16)


def project(attended, table, residual, weights):
    count, channels = attended.shape
    wide = 256
    start = 3 * channels // wide
    whole = lambda array: pl.BlockSpec(array.shape, lambda i: (0, 0))
    column = pl.BlockSpec((count, wide), lambda i: (0, i))
    return pl.pallas_call(
        project_kernel,
        grid=(channels // wide,),
        in_specs=[
            whole(attended),
            whole(table),
            column,
            pl.BlockSpec((channels, wide), lambda i: (0, i + start)),
        ],
        out_specs=column,
        out_shape=jax.ShapeDtypeStruct((count, channels), jnp.bfloat16),
        scratch_shapes=[pltpu.VMEM((count, channels), jnp.bfloat16)],
        cost_estimate=pl.CostEstimate(
            flops=2 * count * channels * 2 * channels,
            bytes_accessed=4 * channels * channels + 6 * count * channels,
            transcendentals=0,
        ),
    )(attended, table, residual, weights)


def shards(latents, timestep, norm_gain, time_weight, conv_weight, attend_weight, output_weight):
    _, frames_dev, pixels, channels = latents.shape
    half = channels // 2
    my = {axis: lax.axis_index(axis) for axis in ALL}
    frame = my["x"] * 4 + my["y"]

    time_slice = lax.dynamic_index_in_dim(time_weight.reshape(20, 16, 80), frame, 1, False)
    piece = jnp.concatenate([attend_weight, output_weight, time_slice.reshape(5, 320)], axis=1)
    steps = range(1, 8)
    stage = jnp.stack([piece] + [shifted(piece, "z", step) for step in steps])
    mixing = stage[:, :, : 4 * channels].reshape(40, 4 * channels)
    mixing = lax.all_gather(mixing, ("core", "x", "y"), axis=0, tiled=True)

    def along(piece_list):
        return jnp.concatenate(piece_list, axis=0)

    taps = jnp.concatenate([conv_weight[t] for t in range(3)], axis=1)
    square = along([p[None] for p in small_ring(taps, "x")])
    square = along(small_ring(square, "y")).reshape(80, 3 * channels)
    pieces = halved_ring(square, "z", 4)
    groups = [along(pieces[:3]), along(pieces[3:5]), along(pieces[5:7]), pieces[7]]
    sides = [[group, shifted(group, "core", 1)] for group in groups]

    values = lax.all_to_all(latents, FRAME, split_axis=2, concat_axis=1, tiled=True)
    values = values.reshape(-1, channels).astype(jnp.float32)

    here = latents.reshape(-1, channels).astype(jnp.float32)
    width = channels // GROUPS
    members = here.shape[0] * width
    mean_here = jnp.sum(jnp.sum(here, axis=0).reshape(GROUPS, width), axis=1) / members
    deviate = here - jnp.repeat(mean_here, width)[None, :]
    square_here = jnp.sum(jnp.sum(deviate * deviate, axis=0).reshape(GROUPS, width), axis=1)
    features = sinusoid(timestep).astype(jnp.bfloat16).reshape(8, 2, 20)
    features = features[(my["z"] - jnp.arange(8)) % 8]
    time_rows = stage[:, :, 4 * channels :].reshape(160, 80)
    time_other = shifted(time_rows, "core", 1)
    bias_here = jnp.zeros((1, 80), jnp.float32)
    for core, rows in ((my["core"], time_rows), (1 - my["core"], time_other)):
        part = lax.dynamic_index_in_dim(features, core, 1, False).reshape(1, 160)
        bias_here = bias_here + jnp.dot(part, rows, preferred_element_type=jnp.float32)
    sums = jnp.concatenate([mean_here, square_here, bias_here[0]])[None, :]
    shifts = [0, -1, -2, -3]
    sums = in_order([sums] + [shifted(sums, "y", s) for s in (1, 2, 3)], "y", shifts)
    sums = in_order([sums] + [shifted(sums, "x", s) for s in (1, 2, 3)], "x", shifts)
    sums = sums.reshape(16, -1)
    means, squares = sums[:, :GROUPS], sums[:, GROUPS : 2 * GROUPS]
    time_bias = sums[:, 2 * GROUPS :].reshape(1, channels)
    center = jnp.mean(means, axis=0)
    spread = jnp.sum(squares, axis=0) + members * jnp.sum((means - center) ** 2, axis=0)
    spread = spread / (16 * members)
    scale = norm_gain / jnp.sqrt(jnp.repeat(spread, width) + 1e-05)
    scaled = (values - jnp.repeat(center, width)[None, :]) * scale[None, :]
    hidden = jax.nn.silu(scaled).astype(jnp.bfloat16)

    spot = jnp.arange(channels, dtype=jnp.int32)
    core, x, y, z, row = digits(spot, (2, 4, 4, 8, 5))
    mixing_table = selection(channel_of((my["z"] - z) % 8, core, x, y, row))
    part, z, y, x, row = digits(spot, (2, 8, 4, 4, 5))
    core = jnp.where(part == 0, my["core"], 1 - my["core"])
    z = (my["z"] + looked_up(z, ring_offsets(4))) % 8
    x = (my["x"] + looked_up(x, [0, -1, 1, -2])) % 4
    y = (my["y"] + looked_up(y, [0, -1, 1, -2])) % 4
    order = channel_of(z, core, x, y, row)

    product = jnp.zeros((values.shape[0], 3 * channels), jnp.float32)
    begin = 0
    for pair in sides:
        depth = pair[0].shape[0]
        for side in range(2):
            at = side * half + begin
            part = moved(hidden, selection(order[at : at + depth]))
            product = product + jnp.dot(part, pair[side], preferred_element_type=jnp.float32)
        begin += depth
    first, middle, last = [product[:, t * channels : (t + 1) * channels] for t in range(3)]
    edge = jnp.zeros((8, channels), jnp.float32)
    before = jnp.concatenate([edge, first[:-8]], axis=0)
    after = jnp.concatenate([last[8:], edge], axis=0)
    conv = before + middle + after + time_bias
    residual = (values + conv).astype(jnp.bfloat16)
    rows = residual.astype(jnp.float32)
    row_mean = jnp.mean(rows, axis=-1, keepdims=True)
    row_var = jnp.mean((rows - row_mean) ** 2, axis=-1, keepdims=True)
    normed = ((rows - row_mean) / jnp.sqrt(row_var + 1e-05)).astype(jnp.bfloat16)
    attended = attend(normed, mixing_table, mixing)
    mixed = project(attended, mixing_table, residual, mixing)
    mixed = mixed.reshape(1, -1, 8, channels)
    return lax.all_to_all(mixed, FRAME, split_axis=1, concat_axis=2, tiled=True)


def solution(mesh):
    split = Mesh(mesh.devices.reshape(8, 2, 4, 4), ALL)
    placed = (
        P(DP, FRAME, None, None),
        P(DP),
        P(),
        P(DP, None),
        P(None, ALL, None),
        P(ALL, None),
        P(ALL, None),
    )
    return jax.shard_map(
        shards, mesh=split, in_specs=placed, out_specs=P(DP, FRAME, None, None), check_vma=False
    )
```

```python
import math

import jax
import jax.numpy as jnp
from jax import lax
from jax.experimental import pallas as pl
from jax.experimental.pallas import tpu as pltpu
from jax.sharding import Mesh
from jax.sharding import PartitionSpec as P


HEADS = 20
HD = 64
GROUPS = 32
TEMB = 320
FRAME = ("x", "y")
DP = ("z", "core")
ALL = ("z", "core", "x", "y")


def shifted(array, axis, step):
    count = lax.axis_size(axis)
    return lax.ppermute(array, axis, [(i, (i + step) % count) for i in range(count)])


def small_ring(piece, axis):
    back = shifted(piece, axis, 1)
    ahead = shifted(piece, axis, -1)
    return [piece, back, ahead, shifted(back, axis, 1)]


def halved_ring(piece, axis, reach):
    pieces = [piece]
    back = ahead = piece
    for _ in range(reach - 1):
        back = shifted(back, axis, 1)
        ahead = shifted(ahead, axis, -1)
        pieces += [back, ahead]
    half = piece.shape[0] // 2
    far = jnp.concatenate(
        [shifted(back[:half], axis, 1), shifted(ahead[half:], axis, -1)], axis=0
    )
    return pieces + [far]


def ring_offsets(reach):
    places = [0]
    for step in range(1, reach):
        places += [-step, step]
    return places + [reach]


def digits(index, sizes):
    out = []
    for size in reversed(sizes):
        out.append(index % size)
        index = index // size
    return out[::-1]


def looked_up(index, table):
    value = jnp.zeros_like(index)
    for place, entry in enumerate(table):
        value = jnp.where(index == place, entry, value)
    return value


def selection(channel):
    source = lax.broadcasted_iota(jnp.int32, (2 * GROUPS * 20, channel.shape[0]), 0)
    return (source == channel[None, :]).astype(jnp.bfloat16)


def channel_of(z, core, x, y, row):
    return z * 160 + core * 80 + x * 20 + y * 5 + row


def moved(array, table):
    return jnp.dot(array, table, preferred_element_type=jnp.float32).astype(jnp.bfloat16)


def in_order(pieces, axis, offsets):
    count = lax.axis_size(axis)
    spots = (lax.axis_index(axis) + jnp.asarray(offsets, jnp.int32)) % count
    pick = (jnp.arange(count)[:, None] == spots[None, :]).astype(jnp.float32)
    stacked = jnp.stack(pieces)
    return jnp.sum(pick.reshape(count, count, *(1,) * (stacked.ndim - 1)) * stacked[None], axis=1)


def sinusoid(timestep):
    half_dim = TEMB // 2
    ladder = jnp.arange(half_dim, dtype=jnp.float32)
    freqs = jnp.exp(-math.log(10000.0) * ladder / half_dim)
    angles = timestep.astype(jnp.float32)[:, None] * freqs[None, :]
    return jnp.concatenate([jnp.cos(angles), jnp.sin(angles)], axis=-1)


def conv_kernel(hidden_ref, values_ref, bias_ref, first_ref, middle_ref, last_ref, out_ref):
    hidden = hidden_ref[...]
    first, middle, last = [
        jnp.dot(hidden, ref[...], preferred_element_type=jnp.float32)
        for ref in (first_ref, middle_ref, last_ref)
    ]
    edge = jnp.zeros((8, first.shape[1]), jnp.float32)
    before = jnp.concatenate([edge, first[:-8]], axis=0)
    after = jnp.concatenate([last[8:], edge], axis=0)
    conv = before + middle + after + bias_ref[...]
    out_ref[...] = (values_ref[...].astype(jnp.float32) + conv).astype(jnp.bfloat16)


def convolve(hidden, values, bias, weights):
    count, channels = hidden.shape
    wide = 256
    blocks = channels // wide
    column = lambda rows, shift: pl.BlockSpec((rows, wide), lambda i: (0, i + shift))
    return pl.pallas_call(
        conv_kernel,
        grid=(blocks,),
        in_specs=[pl.BlockSpec(hidden.shape, lambda i: (0, 0)), column(count, 0), column(1, 0)]
        + [column(channels, tap * blocks) for tap in range(3)],
        out_specs=column(count, 0),
        out_shape=jax.ShapeDtypeStruct((count, channels), jnp.bfloat16),
        cost_estimate=pl.CostEstimate(
            flops=2 * count * channels * 3 * channels,
            bytes_accessed=6 * channels * channels + 6 * count * channels,
            transcendentals=0,
        ),
    )(hidden, values, bias, weights, weights, weights)


def attend_kernel(rows_ref, query_ref, key_ref, value_ref, out_ref, held_ref):
    count = rows_ref.shape[0]
    frames = count // 8

    @pl.when(pl.program_id(0) == 0)
    def _():
        rows = rows_ref[...].astype(jnp.float32)
        centered = rows - jnp.mean(rows, axis=-1, keepdims=True)
        variance = jnp.mean(centered * centered, axis=-1, keepdims=True)
        normed = (centered / jnp.sqrt(variance + 1e-05)).astype(jnp.bfloat16)
        to = lax.broadcasted_iota(jnp.int32, (count, count), 0)
        source = lax.broadcasted_iota(jnp.int32, (count, count), 1)
        by_pixel = (source == (to % frames) * 8 + to // frames).astype(jnp.bfloat16)
        held_ref[...] = moved(by_pixel, normed)

    held = held_ref[...]
    query, key, value = [
        jnp.dot(held, ref[...], preferred_element_type=jnp.float32).astype(jnp.bfloat16)
        for ref in (query_ref, key_ref, value_ref)
    ]
    group = count // 2
    first = lax.broadcasted_iota(jnp.int32, (group, 128), 1) < HD
    same = (
        lax.broadcasted_iota(jnp.int32, (group, group), 0) // frames
        == lax.broadcasted_iota(jnp.int32, (group, group), 1) // frames
    )
    for pair in range(query.shape[1] // 128):
        lanes = slice(pair * 128, (pair + 1) * 128)
        for place in range(2):
            cut = slice(place * group, (place + 1) * group)
            results = []
            for mine in (first, jnp.logical_not(first)):
                part = query[cut, lanes]
                part = jnp.where(mine, part, jnp.zeros_like(part))
                scores = lax.dot_general(
                    part,
                    key[cut, lanes],
                    (((1,), (1,)), ((), ())),
                    preferred_element_type=jnp.float32,
                ) * (1.0 / math.sqrt(HD))
                scores = jnp.where(same, scores, -3e38)
                peak = jnp.max(scores, axis=-1, keepdims=True)
                expo = jnp.exp(scores - peak)
                probs = (expo / jnp.sum(expo, axis=-1, keepdims=True)).astype(jnp.bfloat16)
                results.append(
                    jnp.dot(probs, value[cut, lanes], preferred_element_type=jnp.float32)
                )
            out_ref[cut, lanes] = jnp.where(first, results[0], results[1]).astype(jnp.bfloat16)


def attend(residual, weights):
    count, channels = residual.shape
    wide = 256
    blocks = channels // wide
    block = lambda shift: pl.BlockSpec((channels, wide), lambda i: (0, i + shift))
    return pl.pallas_call(
        attend_kernel,
        grid=(blocks,),
        in_specs=[pl.BlockSpec(residual.shape, lambda i: (0, 0))]
        + [block(0), block(blocks), block(2 * blocks)],
        out_specs=pl.BlockSpec((count, wide), lambda i: (0, i)),
        out_shape=jax.ShapeDtypeStruct((count, channels), jnp.bfloat16),
        scratch_shapes=[pltpu.VMEM((count, channels), jnp.bfloat16)],
        cost_estimate=pl.CostEstimate(
            flops=2 * count * channels * 4 * channels,
            bytes_accessed=6 * channels * channels + 4 * count * channels,
            transcendentals=count * count * HEADS // 2,
        ),
    )(residual, weights, weights, weights)


def project_kernel(attended_ref, table_ref, rows_ref, weight_ref, out_ref, held_ref):
    count = rows_ref.shape[0]
    frames = count // 8

    @pl.when(pl.program_id(0) == 0)
    def _():
        to = lax.broadcasted_iota(jnp.int32, (count, count), 0)
        source = lax.broadcasted_iota(jnp.int32, (count, count), 1)
        by_frame = (source == (to % 8) * frames + to // 8).astype(jnp.bfloat16)
        held_ref[...] = moved(by_frame, moved(attended_ref[...], table_ref[...]))

    product = jnp.dot(held_ref[...], weight_ref[...], preferred_element_type=jnp.float32)
    out_ref[...] = (rows_ref[...].astype(jnp.float32) + product).astype(jnp.bfloat16)


def project(attended, table, residual, weights):
    count, channels = attended.shape
    wide = 256
    start = 3 * channels // wide
    whole = lambda array: pl.BlockSpec(array.shape, lambda i: (0, 0))
    column = pl.BlockSpec((count, wide), lambda i: (0, i))
    return pl.pallas_call(
        project_kernel,
        grid=(channels // wide,),
        in_specs=[
            whole(attended),
            whole(table),
            column,
            pl.BlockSpec((channels, wide), lambda i: (0, i + start)),
        ],
        out_specs=column,
        out_shape=jax.ShapeDtypeStruct((count, channels), jnp.bfloat16),
        scratch_shapes=[pltpu.VMEM((count, channels), jnp.bfloat16)],
        cost_estimate=pl.CostEstimate(
            flops=2 * count * channels * 2 * channels,
            bytes_accessed=4 * channels * channels + 6 * count * channels,
            transcendentals=0,
        ),
    )(attended, table, residual, weights)


def shards(latents, timestep, norm_gain, time_weight, conv_weight, attend_weight, output_weight):
    _, frames_dev, pixels, channels = latents.shape
    my = {axis: lax.axis_index(axis) for axis in ALL}
    frame = my["x"] * 4 + my["y"]

    time_slice = lax.dynamic_index_in_dim(time_weight.reshape(20, 16, 80), frame, 1, False)
    piece = jnp.concatenate(
        [conv_weight[t] for t in range(3)] + [output_weight, time_slice.reshape(5, 320)], axis=1
    ).reshape(-1)
    stage = jnp.stack([piece] + [shifted(piece, "z", step) for step in range(1, 8)])
    stage = stage.reshape(8, 5, -1)
    mixing = stage[:, :, : 4 * channels].reshape(40, 4 * channels)
    attend_weight, mixing = lax.optimization_barrier((attend_weight, mixing))
    mixing = lax.all_gather(mixing, ("core", "x", "y"), axis=0, tiled=True)

    square = attend_weight
    for axis in ("y", "x"):
        held = jnp.zeros((4, *square.shape), square.dtype)
        for offset, part in zip((0, -1, 1, -2), small_ring(square, axis)):
            held = lax.dynamic_update_index_in_dim(held, part, (my[axis] + offset) % 4, 0)
        square = held
    square = square.reshape(80, 3 * channels)
    latents, time_weight, stage, square = lax.optimization_barrier(
        (latents, time_weight, stage, square)
    )
    attending = jnp.zeros((16, 80, 3 * channels), square.dtype)
    for offset, part in zip(ring_offsets(4), halved_ring(square, "z", 4)):
        place = (my["z"] + offset) % 8 * 2
        attending = lax.dynamic_update_index_in_dim(attending, part, place + my["core"], 0)
        other = shifted(part, "core", 1)
        attending = lax.dynamic_update_index_in_dim(attending, other, place + 1 - my["core"], 0)
    attending = attending.reshape(channels, 3 * channels)

    values = lax.all_to_all(latents, FRAME, split_axis=2, concat_axis=1, tiled=True)
    values = values.reshape(-1, channels)

    here = latents.reshape(-1, channels).astype(jnp.float32)
    width = channels // GROUPS
    members = here.shape[0] * width
    mean_here = jnp.sum(jnp.sum(here, axis=0).reshape(GROUPS, width), axis=1) / members
    deviate = here - jnp.repeat(mean_here, width)[None, :]
    square_here = jnp.sum(jnp.sum(deviate * deviate, axis=0).reshape(GROUPS, width), axis=1)
    features = sinusoid(timestep).astype(jnp.bfloat16).reshape(8, 2, 20)
    features = features[(my["z"] - jnp.arange(8)) % 8]
    time_rows = stage[:, :, 4 * channels :].reshape(160, 80)
    time_other = shifted(time_rows, "core", 1)
    bias_here = jnp.zeros((1, 80), jnp.float32)
    for core, rows in ((my["core"], time_rows), (1 - my["core"], time_other)):
        part = lax.dynamic_index_in_dim(features, core, 1, False).reshape(1, 160)
        bias_here = bias_here + jnp.dot(part, rows, preferred_element_type=jnp.float32)
    sums = jnp.concatenate([mean_here, square_here, bias_here[0]])[None, :]
    shifts = [0, -1, -2, -3]
    sums = in_order([sums] + [shifted(sums, "y", s) for s in (1, 2, 3)], "y", shifts)
    sums = in_order([sums] + [shifted(sums, "x", s) for s in (1, 2, 3)], "x", shifts)
    sums = sums.reshape(16, -1)
    means, squares = sums[:, :GROUPS], sums[:, GROUPS : 2 * GROUPS]
    time_bias = sums[:, 2 * GROUPS :].reshape(1, channels)
    center = jnp.mean(means, axis=0)
    spread = jnp.sum(squares, axis=0) + members * jnp.sum((means - center) ** 2, axis=0)
    spread = spread / (16 * members)
    scale = norm_gain / jnp.sqrt(jnp.repeat(spread, width) + 1e-05)
    scaled = (values.astype(jnp.float32) - jnp.repeat(center, width)[None, :]) * scale[None, :]
    hidden = jax.nn.silu(scaled).astype(jnp.bfloat16)

    spot = jnp.arange(channels, dtype=jnp.int32)
    core, x, y, z, row = digits(spot, (2, 4, 4, 8, 5))
    mixing_table = selection(channel_of((my["z"] - z) % 8, core, x, y, row))

    residual = convolve(moved(hidden, mixing_table), values, time_bias, mixing)
    attended = attend(residual, attending)
    mixed = project(attended, mixing_table, residual, mixing)
    mixed = mixed.reshape(1, -1, 8, channels)
    return lax.all_to_all(mixed, FRAME, split_axis=1, concat_axis=2, tiled=True)


def solution(mesh):
    split = Mesh(mesh.devices.reshape(8, 2, 4, 4), ALL)
    placed = (
        P(DP, FRAME, None, None),
        P(DP),
        P(),
        P(DP, None),
        P(None, ALL, None),
        P(ALL, None),
        P(ALL, None),
    )
    return jax.shard_map(
        shards, mesh=split, in_specs=placed, out_specs=P(DP, FRAME, None, None), check_vma=False
    )
```

```python
import math

import jax
import jax.numpy as jnp
from jax import lax
from jax.experimental import pallas as pl
from jax.experimental.pallas import tpu as pltpu
from jax.sharding import Mesh
from jax.sharding import PartitionSpec as P


HEADS = 20
HD = 64
GROUPS = 32
TEMB = 320
FRAME = ("x", "y")
DP = ("z", "core")
ALL = ("z", "core", "x", "y")


def shifted(array, axis, step):
    count = lax.axis_size(axis)
    return lax.ppermute(array, axis, [(i, (i + step) % count) for i in range(count)])


def ring(piece, axis, reach):
    pieces = [piece]
    back = ahead = piece
    for _ in range(reach - 1):
        back = shifted(back, axis, 1)
        ahead = shifted(ahead, axis, -1)
        pieces += [back, ahead]
    return pieces + [shifted(back, axis, 1)]


def ring_offsets(reach):
    places = [0]
    for step in range(1, reach):
        places += [-step, step]
    return places + [reach]


def digits(index, sizes):
    out = []
    for size in reversed(sizes):
        out.append(index % size)
        index = index // size
    return out[::-1]


def looked_up(index, table):
    value = jnp.zeros_like(index)
    for place, entry in enumerate(table):
        value = jnp.where(index == place, entry, value)
    return value


def selection(channel):
    source = lax.broadcasted_iota(jnp.int32, (2 * GROUPS * 20, channel.shape[0]), 0)
    return (source == channel[None, :]).astype(jnp.bfloat16)


def channel_of(z, core, x, y, row):
    return z * 160 + core * 80 + x * 20 + y * 5 + row


def moved(array, table):
    return jnp.dot(array, table, preferred_element_type=jnp.float32).astype(jnp.bfloat16)


def in_order(pieces, axis, offsets):
    count = lax.axis_size(axis)
    spots = (lax.axis_index(axis) + jnp.asarray(offsets, jnp.int32)) % count
    pick = (jnp.arange(count)[:, None] == spots[None, :]).astype(jnp.float32)
    stacked = jnp.stack(pieces)
    return jnp.sum(pick.reshape(count, count, *(1,) * (stacked.ndim - 1)) * stacked[None], axis=1)


def sinusoid(timestep):
    half_dim = TEMB // 2
    ladder = jnp.arange(half_dim, dtype=jnp.float32)
    freqs = jnp.exp(-math.log(10000.0) * ladder / half_dim)
    angles = timestep.astype(jnp.float32)[:, None] * freqs[None, :]
    return jnp.concatenate([jnp.cos(angles), jnp.sin(angles)], axis=-1)


def conv_kernel(hidden_ref, values_ref, bias_ref, first_ref, middle_ref, last_ref, out_ref):
    hidden = hidden_ref[...]
    first, middle, last = [
        jnp.dot(hidden, ref[...], preferred_element_type=jnp.float32)
        for ref in (first_ref, middle_ref, last_ref)
    ]
    edge = jnp.zeros((8, first.shape[1]), jnp.float32)
    before = jnp.concatenate([edge, first[:-8]], axis=0)
    after = jnp.concatenate([last[8:], edge], axis=0)
    conv = before + middle + after + bias_ref[...]
    out_ref[...] = (values_ref[...].astype(jnp.float32) + conv).astype(jnp.bfloat16)


def convolve(hidden, values, bias, weights):
    count, channels = hidden.shape
    wide = 256
    blocks = channels // wide
    column = lambda rows, shift: pl.BlockSpec((rows, wide), lambda i: (0, i + shift))
    return pl.pallas_call(
        conv_kernel,
        grid=(blocks,),
        in_specs=[pl.BlockSpec(hidden.shape, lambda i: (0, 0)), column(count, 0), column(1, 0)]
        + [column(channels, tap * blocks) for tap in range(3)],
        out_specs=column(count, 0),
        out_shape=jax.ShapeDtypeStruct((count, channels), jnp.bfloat16),
        cost_estimate=pl.CostEstimate(
            flops=2 * count * channels * 3 * channels,
            bytes_accessed=6 * channels * channels + 6 * count * channels,
            transcendentals=0,
        ),
    )(hidden, values, bias, weights, weights, weights)


def attend_kernel(rows_ref, table_ref, query_ref, key_ref, value_ref, out_ref, held_ref):
    count = rows_ref.shape[0]
    frames = count // 8

    @pl.when(pl.program_id(0) == 0)
    def _():
        rows = rows_ref[...].astype(jnp.float32)
        centered = rows - jnp.mean(rows, axis=-1, keepdims=True)
        variance = jnp.mean(centered * centered, axis=-1, keepdims=True)
        normed = (centered / jnp.sqrt(variance + 1e-05)).astype(jnp.bfloat16)
        to = lax.broadcasted_iota(jnp.int32, (count, count), 0)
        source = lax.broadcasted_iota(jnp.int32, (count, count), 1)
        by_pixel = (source == (to % frames) * 8 + to // frames).astype(jnp.bfloat16)
        held_ref[...] = moved(by_pixel, moved(normed, table_ref[...]))

    held = held_ref[...]
    query, key, value = [
        jnp.dot(held, ref[...], preferred_element_type=jnp.float32).astype(jnp.bfloat16)
        for ref in (query_ref, key_ref, value_ref)
    ]
    group = count // 2
    first = lax.broadcasted_iota(jnp.int32, (group, 128), 1) < HD
    same = (
        lax.broadcasted_iota(jnp.int32, (group, group), 0) // frames
        == lax.broadcasted_iota(jnp.int32, (group, group), 1) // frames
    )
    for pair in range(query.shape[1] // 128):
        lanes = slice(pair * 128, (pair + 1) * 128)
        for place in range(2):
            cut = slice(place * group, (place + 1) * group)
            results = []
            for mine in (first, jnp.logical_not(first)):
                part = query[cut, lanes]
                part = jnp.where(mine, part, jnp.zeros_like(part))
                scores = lax.dot_general(
                    part,
                    key[cut, lanes],
                    (((1,), (1,)), ((), ())),
                    preferred_element_type=jnp.float32,
                ) * (1.0 / math.sqrt(HD))
                scores = jnp.where(same, scores, -3e38)
                peak = jnp.max(scores, axis=-1, keepdims=True)
                expo = jnp.exp(scores - peak)
                probs = (expo / jnp.sum(expo, axis=-1, keepdims=True)).astype(jnp.bfloat16)
                results.append(
                    jnp.dot(probs, value[cut, lanes], preferred_element_type=jnp.float32)
                )
            out_ref[cut, lanes] = jnp.where(first, results[0], results[1]).astype(jnp.bfloat16)


def attend(residual, table, weights):
    count, channels = residual.shape
    wide = 256
    blocks = channels // wide
    whole = lambda array: pl.BlockSpec(array.shape, lambda i: (0, 0))
    block = lambda part: pl.BlockSpec((channels, wide), lambda i: (0, i + part * blocks))
    return pl.pallas_call(
        attend_kernel,
        grid=(blocks,),
        in_specs=[whole(residual), whole(table), block(3), block(4), block(5)],
        out_specs=pl.BlockSpec((count, wide), lambda i: (0, i)),
        out_shape=jax.ShapeDtypeStruct((count, channels), jnp.bfloat16),
        scratch_shapes=[pltpu.VMEM((count, channels), jnp.bfloat16)],
        cost_estimate=pl.CostEstimate(
            flops=2 * count * channels * 4 * channels,
            bytes_accessed=6 * channels * channels + 4 * count * channels,
            transcendentals=count * count * HEADS // 2,
        ),
    )(residual, table, weights, weights, weights)


def project_kernel(attended_ref, table_ref, rows_ref, weight_ref, out_ref, held_ref):
    count = rows_ref.shape[0]
    frames = count // 8

    @pl.when(pl.program_id(0) == 0)
    def _():
        to = lax.broadcasted_iota(jnp.int32, (count, count), 0)
        source = lax.broadcasted_iota(jnp.int32, (count, count), 1)
        by_frame = (source == (to % 8) * frames + to // 8).astype(jnp.bfloat16)
        held_ref[...] = moved(by_frame, moved(attended_ref[...], table_ref[...]))

    product = jnp.dot(held_ref[...], weight_ref[...], preferred_element_type=jnp.float32)
    out_ref[...] = (rows_ref[...].astype(jnp.float32) + product).astype(jnp.bfloat16)


def project(attended, table, residual, weights):
    count, channels = attended.shape
    wide = 256
    start = 6 * channels // wide
    whole = lambda array: pl.BlockSpec(array.shape, lambda i: (0, 0))
    column = pl.BlockSpec((count, wide), lambda i: (0, i))
    return pl.pallas_call(
        project_kernel,
        grid=(channels // wide,),
        in_specs=[
            whole(attended),
            whole(table),
            column,
            pl.BlockSpec((channels, wide), lambda i: (0, i + start)),
        ],
        out_specs=column,
        out_shape=jax.ShapeDtypeStruct((count, channels), jnp.bfloat16),
        scratch_shapes=[pltpu.VMEM((count, channels), jnp.bfloat16)],
        cost_estimate=pl.CostEstimate(
            flops=2 * count * channels * 2 * channels,
            bytes_accessed=4 * channels * channels + 6 * count * channels,
            transcendentals=0,
        ),
    )(attended, table, residual, weights)


def shards(latents, timestep, norm_gain, time_weight, conv_weight, attend_weight, output_weight):
    _, frames_dev, pixels, channels = latents.shape
    my = {axis: lax.axis_index(axis) for axis in ALL}
    frame = my["x"] * 4 + my["y"]

    time_slice = lax.dynamic_index_in_dim(time_weight.reshape(20, 16, 80), frame, 1, False)
    piece = jnp.concatenate(
        [conv_weight[t] for t in range(3)]
        + [attend_weight, output_weight, time_slice.reshape(5, 320)],
        axis=1,
    ).reshape(-1)
    stage = jnp.stack(ring(piece, "z", 4)).reshape(8, 5, -1)
    mixing = stage[:, :, : 7 * channels].reshape(40, 7 * channels)
    mixing = lax.all_gather(mixing, ("core", "x", "y"), axis=0, tiled=True)
    latents, stage = lax.optimization_barrier((latents, stage))

    values = lax.all_to_all(latents, FRAME, split_axis=2, concat_axis=1, tiled=True)
    values = values.reshape(-1, channels)

    here = latents.reshape(-1, channels).astype(jnp.float32)
    width = channels // GROUPS
    members = here.shape[0] * width
    mean_here = jnp.sum(jnp.sum(here, axis=0).reshape(GROUPS, width), axis=1) / members
    deviate = here - jnp.repeat(mean_here, width)[None, :]
    square_here = jnp.sum(jnp.sum(deviate * deviate, axis=0).reshape(GROUPS, width), axis=1)
    features = sinusoid(timestep).astype(jnp.bfloat16).reshape(8, 2, 20)
    features = features[(my["z"] + jnp.asarray(ring_offsets(4))) % 8]
    time_rows = stage[:, :, 7 * channels :].reshape(160, 80)
    time_other = shifted(time_rows, "core", 1)
    bias_here = jnp.zeros((1, 80), jnp.float32)
    for core, rows in ((my["core"], time_rows), (1 - my["core"], time_other)):
        part = lax.dynamic_index_in_dim(features, core, 1, False).reshape(1, 160)
        bias_here = bias_here + jnp.dot(part, rows, preferred_element_type=jnp.float32)
    sums = jnp.concatenate([mean_here, square_here, bias_here[0]])[None, :]
    shifts = [0, -1, -2, -3]
    sums = in_order([sums] + [shifted(sums, "y", s) for s in (1, 2, 3)], "y", shifts)
    sums = in_order([sums] + [shifted(sums, "x", s) for s in (1, 2, 3)], "x", shifts)
    sums = sums.reshape(16, -1)
    means, squares = sums[:, :GROUPS], sums[:, GROUPS : 2 * GROUPS]
    time_bias = sums[:, 2 * GROUPS :].reshape(1, channels)
    center = jnp.mean(means, axis=0)
    spread = jnp.sum(squares, axis=0) + members * jnp.sum((means - center) ** 2, axis=0)
    spread = spread / (16 * members)
    scale = norm_gain / jnp.sqrt(jnp.repeat(spread, width) + 1e-05)
    scaled = (values.astype(jnp.float32) - jnp.repeat(center, width)[None, :]) * scale[None, :]
    hidden = jax.nn.silu(scaled).astype(jnp.bfloat16)

    spot = jnp.arange(channels, dtype=jnp.int32)
    core, x, y, z, row = digits(spot, (2, 4, 4, 8, 5))
    mixing_table = selection(channel_of((my["z"] + looked_up(z, ring_offsets(4))) % 8, core, x, y, row))

    residual = convolve(moved(hidden, mixing_table), values, time_bias, mixing)
    attended = attend(residual, mixing_table, mixing)
    mixed = project(attended, mixing_table, residual, mixing)
    mixed = mixed.reshape(1, -1, 8, channels)
    return lax.all_to_all(mixed, FRAME, split_axis=1, concat_axis=2, tiled=True)


def solution(mesh):
    split = Mesh(mesh.devices.reshape(8, 2, 4, 4), ALL)
    placed = (
        P(DP, FRAME, None, None),
        P(DP),
        P(),
        P(DP, None),
        P(None, ALL, None),
        P(ALL, None),
        P(ALL, None),
    )
    return jax.shard_map(
        shards, mesh=split, in_specs=placed, out_specs=P(DP, FRAME, None, None), check_vma=False
    )
```

```python
import math

import jax
import jax.numpy as jnp
from jax import lax
from jax.experimental import pallas as pl
from jax.experimental.pallas import tpu as pltpu
from jax.sharding import Mesh
from jax.sharding import PartitionSpec as P


HEADS = 20
HD = 64
GROUPS = 32
TEMB = 320
FRAME = ("x", "y")
DP = ("z", "core")
ALL = ("z", "core", "x", "y")


def shifted(array, axis, step):
    count = lax.axis_size(axis)
    return lax.ppermute(array, axis, [(i, (i + step) % count) for i in range(count)])


RING = (0, 1, -1, 2, -2, 3, -3, 4)


def ring(piece, axis):
    near = [shifted(piece, axis, step) for step in RING[1:5]]
    return [piece] + near + [
        shifted(near[2], axis, 1),
        shifted(near[3], axis, -1),
        shifted(near[2], axis, 2),
    ]


def digits(index, sizes):
    out = []
    for size in reversed(sizes):
        out.append(index % size)
        index = index // size
    return out[::-1]


def looked_up(index, table):
    value = jnp.zeros_like(index)
    for place, entry in enumerate(table):
        value = jnp.where(index == place, entry, value)
    return value


def selection(channel):
    source = lax.broadcasted_iota(jnp.int32, (2 * GROUPS * 20, channel.shape[0]), 0)
    return (source == channel[None, :]).astype(jnp.bfloat16)


def channel_of(z, core, x, y, row):
    return z * 160 + core * 80 + x * 20 + y * 5 + row


def moved(array, table):
    return jnp.dot(array, table, preferred_element_type=jnp.float32).astype(jnp.bfloat16)


def in_order(pieces, axis, offsets):
    count = lax.axis_size(axis)
    spots = (lax.axis_index(axis) + jnp.asarray(offsets, jnp.int32)) % count
    pick = (jnp.arange(count)[:, None] == spots[None, :]).astype(jnp.float32)
    stacked = jnp.stack(pieces)
    return jnp.sum(pick.reshape(count, count, *(1,) * (stacked.ndim - 1)) * stacked[None], axis=1)


def sinusoid(timestep):
    half_dim = TEMB // 2
    ladder = jnp.arange(half_dim, dtype=jnp.float32)
    freqs = jnp.exp(-math.log(10000.0) * ladder / half_dim)
    angles = timestep.astype(jnp.float32)[:, None] * freqs[None, :]
    return jnp.concatenate([jnp.cos(angles), jnp.sin(angles)], axis=-1)


def attended_pair(query, key, value, first, same):
    results = []
    for mine in (first, jnp.logical_not(first)):
        part = jnp.where(mine, query, jnp.zeros_like(query)) * (1.0 / math.sqrt(HD))
        scores = lax.dot_general(
            part.astype(jnp.bfloat16),
            key,
            (((1,), (1,)), ((), ())),
            preferred_element_type=jnp.float32,
        )
        scores = jnp.where(same, scores, -3e38)
        expo = jnp.exp(scores - jnp.max(scores, axis=-1, keepdims=True)).astype(jnp.bfloat16)
        padded = jnp.where(mine, value, jnp.ones_like(value))
        results.append(jnp.dot(expo, padded, preferred_element_type=jnp.float32))
    sums = pltpu.roll(jnp.where(first, results[1], results[0]), HD, 1)
    return (jnp.where(first, results[0], results[1]) / sums).astype(jnp.bfloat16)


WIDE = 256


def block_kernel(
    hidden_ref, values_ref, bias_ref, order_ref, first_ref, middle_ref, last_ref, out_ref,
    table_ref, residual_ref, held_ref, attended_ref
):
    count, channels = hidden_ref.shape
    frames = count // 8
    blocks = channels // WIDE
    step = pl.program_id(0)
    product = lambda left, right: jnp.dot(left, right, preferred_element_type=jnp.float32)
    to = lax.broadcasted_iota(jnp.int32, (count, count), 0)
    source = lax.broadcasted_iota(jnp.int32, (count, count), 1)

    @pl.when(step < blocks)
    def _():
        lanes = pl.ds(pl.multiple_of(step * WIDE, WIDE), WIDE)
        hidden = hidden_ref[...]
        first, middle, last = [
            product(hidden, ref[...]) for ref in (first_ref, middle_ref, last_ref)
        ]
        edge = jnp.zeros((8, WIDE), jnp.float32)
        before = jnp.concatenate([edge, first[:-8]], axis=0)
        after = jnp.concatenate([last[8:], edge], axis=0)
        conv = before + middle + after + bias_ref[:, lanes]
        residual_ref[:, lanes] = (values_ref[:, lanes].astype(jnp.float32) + conv).astype(
            jnp.bfloat16
        )
        channel = lax.broadcasted_iota(jnp.int32, (channels, WIDE), 0)
        table_ref[:, lanes] = (channel == order_ref[:, lanes]).astype(jnp.bfloat16)

    @pl.when(step == blocks)
    def _():
        rows = residual_ref[...].astype(jnp.float32)
        centered = rows - jnp.mean(rows, axis=-1, keepdims=True)
        variance = jnp.mean(centered * centered, axis=-1, keepdims=True)
        normed = (centered / jnp.sqrt(variance + 1e-05)).astype(jnp.bfloat16)
        by_pixel = (source == (to % frames) * 8 + to // frames).astype(jnp.bfloat16)
        held_ref[...] = moved(by_pixel, moved(normed, table_ref[...]))

    @pl.when(jnp.logical_and(step >= blocks, step < 2 * blocks))
    def _():
        held = held_ref[...]
        query, key, value = [
            product(held, ref[...]).astype(jnp.bfloat16)
            for ref in (first_ref, middle_ref, last_ref)
        ]
        group = count // 2
        first = lax.broadcasted_iota(jnp.int32, (group, 128), 1) < HD
        same = (
            lax.broadcasted_iota(jnp.int32, (group, group), 0) // frames
            == lax.broadcasted_iota(jnp.int32, (group, group), 1) // frames
        )
        halves = []
        for place in range(2):
            cut = slice(place * group, (place + 1) * group)
            pairs = []
            for pair in range(WIDE // 128):
                lanes = slice(pair * 128, (pair + 1) * 128)
                pairs.append(
                    attended_pair(
                        query[cut, lanes], key[cut, lanes], value[cut, lanes], first, same
                    )
                )
            halves.append(jnp.concatenate(pairs, axis=1))
        lanes = pl.ds(pl.multiple_of((step - blocks) * WIDE, WIDE), WIDE)
        attended_ref[:, lanes] = jnp.concatenate(halves, axis=0)

    @pl.when(step == 2 * blocks)
    def _():
        by_frame = (source == (to % 8) * frames + to // 8).astype(jnp.bfloat16)
        held_ref[...] = moved(by_frame, moved(attended_ref[...], table_ref[...]))

    @pl.when(step >= 2 * blocks)
    def _():
        lanes = pl.ds(pl.multiple_of((step - 2 * blocks) * WIDE, WIDE), WIDE)
        rows = residual_ref[:, lanes].astype(jnp.float32)
        out_ref[...] = (rows + product(held_ref[...], first_ref[...])).astype(jnp.bfloat16)


def block(hidden, values, bias, order, weights):
    count, channels = hidden.shape
    blocks = channels // WIDE
    whole = lambda array: pl.BlockSpec(array.shape, lambda i: (0, 0))

    def weight(part):
        def at(i):
            inner = jnp.where(i < blocks, i, i + 2 * blocks) + part * blocks
            tail = i + 4 * blocks if part == 0 else (3 + part) * blocks + blocks - 1
            return 0, jnp.where(i < 2 * blocks, inner, tail)

        return pl.BlockSpec((channels, WIDE), at)

    return pl.pallas_call(
        block_kernel,
        grid=(3 * blocks,),
        in_specs=[whole(hidden), whole(values), whole(bias), whole(order)]
        + [weight(part) for part in range(3)],
        out_specs=pl.BlockSpec((count, WIDE), lambda i: (0, jnp.maximum(i - 2 * blocks, 0))),
        out_shape=jax.ShapeDtypeStruct((count, channels), jnp.bfloat16),
        scratch_shapes=[pltpu.VMEM((channels, channels), jnp.bfloat16)]
        + [pltpu.VMEM((count, channels), jnp.bfloat16)] * 3,
        cost_estimate=pl.CostEstimate(
            flops=2 * count * channels * 9 * channels,
            bytes_accessed=14 * channels * channels + 8 * count * channels,
            transcendentals=count * count * HEADS // 2,
        ),
    )(hidden, values, bias, order, weights, weights, weights)


def shards(latents, timestep, norm_gain, time_weight, conv_weight, attend_weight, output_weight):
    _, frames_dev, pixels, channels = latents.shape
    my = {axis: lax.axis_index(axis) for axis in ALL}
    frame = my["x"] * 4 + my["y"]

    time_slice = lax.dynamic_index_in_dim(time_weight.reshape(20, 16, 80), frame, 1, False)
    piece = jnp.concatenate(
        [conv_weight[t] for t in range(3)]
        + [attend_weight, output_weight, time_slice.reshape(5, 320)],
        axis=1,
    ).reshape(-1)
    stage = jnp.stack(ring(piece, "z")).reshape(8, 5, -1)
    mixing = stage[:, :, : 7 * channels].reshape(40, 7 * channels)
    mixing = lax.all_gather(mixing, ("core", "x", "y"), axis=0, tiled=True)
    latents, stage = lax.optimization_barrier((latents, stage))

    values = lax.all_to_all(latents, FRAME, split_axis=2, concat_axis=1, tiled=True)
    values = values.reshape(-1, channels)

    here = latents.reshape(-1, channels).astype(jnp.float32)
    width = channels // GROUPS
    members = here.shape[0] * width
    mean_here = jnp.sum(jnp.sum(here, axis=0).reshape(GROUPS, width), axis=1) / members
    deviate = here - jnp.repeat(mean_here, width)[None, :]
    square_here = jnp.sum(jnp.sum(deviate * deviate, axis=0).reshape(GROUPS, width), axis=1)
    features = sinusoid(timestep).astype(jnp.bfloat16).reshape(8, 2, 20)
    features = features[(my["z"] - jnp.asarray(RING)) % 8]
    time_rows = stage[:, :, 7 * channels :].reshape(160, 80)
    time_other = shifted(time_rows, "core", 1)
    bias_here = jnp.zeros((1, 80), jnp.float32)
    for core, rows in ((my["core"], time_rows), (1 - my["core"], time_other)):
        part = lax.dynamic_index_in_dim(features, core, 1, False).reshape(1, 160)
        bias_here = bias_here + jnp.dot(part, rows, preferred_element_type=jnp.float32)
    sums = jnp.concatenate([mean_here, square_here, bias_here[0]])[None, :]
    shifts = [0, -1, -2, -3]
    sums = in_order([sums] + [shifted(sums, "y", s) for s in (1, 2, 3)], "y", shifts)
    sums = in_order([sums] + [shifted(sums, "x", s) for s in (1, 2, 3)], "x", shifts)
    sums = sums.reshape(16, -1)
    means, squares = sums[:, :GROUPS], sums[:, GROUPS : 2 * GROUPS]
    time_bias = sums[:, 2 * GROUPS :].reshape(1, channels)
    center = jnp.mean(means, axis=0)
    spread = jnp.sum(squares, axis=0) + members * jnp.sum((means - center) ** 2, axis=0)
    spread = spread / (16 * members)
    scale = norm_gain / jnp.sqrt(jnp.repeat(spread, width) + 1e-05)
    scaled = (values.astype(jnp.float32) - jnp.repeat(center, width)[None, :]) * scale[None, :]
    hidden = jax.nn.silu(scaled).astype(jnp.bfloat16)

    spot = jnp.arange(channels, dtype=jnp.int32)
    core, x, y, z, row = digits(spot, (2, 4, 4, 8, 5))
    order = channel_of((my["z"] - looked_up(z, RING)) % 8, core, x, y, row)

    hidden = moved(hidden, selection(order))
    mixed = block(hidden, values, time_bias, order[None, :], mixing)
    mixed = mixed.reshape(1, -1, 8, channels)
    return lax.all_to_all(mixed, FRAME, split_axis=1, concat_axis=2, tiled=True)


def solution(mesh):
    split = Mesh(mesh.devices.reshape(8, 2, 4, 4), ALL)
    placed = (
        P(DP, FRAME, None, None),
        P(DP),
        P(),
        P(DP, None),
        P(None, ALL, None),
        P(ALL, None),
        P(ALL, None),
    )
    return jax.shard_map(
        shards, mesh=split, in_specs=placed, out_specs=P(DP, FRAME, None, None), check_vma=False
    )
```

```python
import math

import jax
import jax.numpy as jnp
import numpy as np
from jax import lax
from jax.experimental import pallas as pl
from jax.experimental.pallas import tpu as pltpu
from jax.sharding import Mesh
from jax.sharding import PartitionSpec as P


HEADS = 20
HD = 64
GROUPS = 32
TEMB = 320
FRAME = ("x", "y")
DP = ("z", "core")
ALL = ("z", "core", "x", "y")


def shifted(array, axis, step):
    count = lax.axis_size(axis)
    return lax.ppermute(array, axis, [(i, (i + step) % count) for i in range(count)])


RING = (0, 1, -1, 2, -2, 3, -3, 4)
SMALL = (0, 1, -1, 2)


def channel_of(z, core, x, y, row):
    return z * 160 + core * 80 + x * 20 + y * 5 + row


def moved(array, table):
    return jnp.dot(array, table, preferred_element_type=jnp.float32).astype(jnp.bfloat16)


def sinusoid(timestep):
    half_dim = TEMB // 2
    ladder = jnp.arange(half_dim, dtype=jnp.float32)
    freqs = jnp.exp(-math.log(10000.0) * ladder / half_dim)
    angles = timestep.astype(jnp.float32)[:, None] * freqs[None, :]
    return jnp.concatenate([jnp.cos(angles), jnp.sin(angles)], axis=-1)


def attended_pair(query, key, value, first, same):
    results = []
    for mine in (first, jnp.logical_not(first)):
        part = jnp.where(mine, query, jnp.zeros_like(query)) * (1.0 / math.sqrt(HD))
        scores = lax.dot_general(
            part.astype(jnp.bfloat16),
            key,
            (((1,), (1,)), ((), ())),
            preferred_element_type=jnp.float32,
        )
        scores = jnp.where(same, scores, -3e38)
        expo = jnp.exp(scores - jnp.max(scores, axis=-1, keepdims=True)).astype(jnp.bfloat16)
        padded = jnp.where(mine, value, jnp.ones_like(value))
        results.append(jnp.dot(expo, padded, preferred_element_type=jnp.float32))
    sums = pltpu.roll(jnp.where(first, results[1], results[0]), HD, 1)
    return (jnp.where(first, results[0], results[1]) / sums).astype(jnp.bfloat16)


WIDE = 256
PADDED = 1536
PARTS = ((0, 640), (768, 640))


def fill(table_ref, order_ref, lanes):
    order = order_ref[:, lanes]
    channel = lax.broadcasted_iota(jnp.int32, (table_ref.shape[0], order.shape[1]), 0)
    table_ref[:, lanes] = (channel == order).astype(jnp.bfloat16)


def block_kernel(
    hidden_ref, values_ref, bias_ref, order_ref, attend_order_ref,
    first_ref, middle_ref, last_ref, *refs
):
    attend_refs, refs = refs[: 3 * len(PARTS)], refs[3 * len(PARTS) :]
    out_ref, table_ref, attend_table_ref, residual_ref, mixed_ref, held_ref, attended_ref = refs
    count, channels = hidden_ref.shape
    frames = count // 8
    blocks = channels // WIDE
    step = pl.program_id(0)
    product = lambda left, right: jnp.dot(left, right, preferred_element_type=jnp.float32)
    to = lax.broadcasted_iota(jnp.int32, (count, count), 0)
    source = lax.broadcasted_iota(jnp.int32, (count, count), 1)

    @pl.when(step < blocks)
    def _():
        lanes = pl.ds(pl.multiple_of(step * WIDE, WIDE), WIDE)
        hidden = hidden_ref[...]
        first, middle, last = [
            product(hidden, ref[...]) for ref in (first_ref, middle_ref, last_ref)
        ]
        edge = jnp.zeros((8, WIDE), jnp.float32)
        before = jnp.concatenate([edge, first[:-8]], axis=0)
        after = jnp.concatenate([last[8:], edge], axis=0)
        conv = before + middle + after + bias_ref[:, lanes]
        residual_ref[:, lanes] = (values_ref[:, lanes].astype(jnp.float32) + conv).astype(
            jnp.bfloat16
        )
        fill(attend_table_ref, attend_order_ref, lanes)

    @pl.when(step == 0)
    def _():
        fill(attend_table_ref, attend_order_ref, slice(channels, PADDED))

    @pl.when(step == blocks)
    def _():
        rows = residual_ref[...].astype(jnp.float32)
        centered = rows - jnp.mean(rows, axis=-1, keepdims=True)
        variance = jnp.mean(centered * centered, axis=-1, keepdims=True)
        normed = (centered / jnp.sqrt(variance + 1e-05)).astype(jnp.bfloat16)
        by_pixel = (source == (to % frames) * 8 + to // frames).astype(jnp.bfloat16)
        held_ref[...] = moved(by_pixel, normed)

        @pl.loop(0, PADDED // WIDE)
        def _(part):
            lanes = pl.ds(pl.multiple_of(part * WIDE, WIDE), WIDE)
            mixed_ref[:, lanes] = moved(held_ref[...], attend_table_ref[:, lanes])

    @pl.when(jnp.logical_and(step >= blocks, step < 2 * blocks))
    def _():
        triple = []
        for which in range(3):
            total = 0.0
            for part, (at, depth) in enumerate(PARTS):
                weight = attend_refs[part * 3 + which][...]
                total = total + product(mixed_ref[:, at : at + depth], weight)
            triple.append(total.astype(jnp.bfloat16))
        query, key, value = triple
        group = count // 2
        first = lax.broadcasted_iota(jnp.int32, (group, 128), 1) < HD
        same = (
            lax.broadcasted_iota(jnp.int32, (group, group), 0) // frames
            == lax.broadcasted_iota(jnp.int32, (group, group), 1) // frames
        )
        base = (step - blocks) * WIDE
        for place in range(2):
            cut = slice(place * group, (place + 1) * group)
            for pair in range(WIDE // 128):
                lanes = slice(pair * 128, (pair + 1) * 128)
                target = pl.ds(pl.multiple_of(base + pair * 128, 128), 128)
                attended_ref[cut, target] = attended_pair(
                    query[cut, lanes], key[cut, lanes], value[cut, lanes], first, same
                )
        lanes = pl.ds(pl.multiple_of(base, WIDE), WIDE)
        fill(table_ref, order_ref, lanes)

    @pl.when(step == 2 * blocks)
    def _():
        by_frame = (source == (to % 8) * frames + to // 8).astype(jnp.bfloat16)
        mixed_ref[:, :channels] = moved(by_frame, attended_ref[...])

        @pl.loop(0, blocks)
        def _(part):
            lanes = pl.ds(pl.multiple_of(part * WIDE, WIDE), WIDE)
            held_ref[:, lanes] = moved(mixed_ref[:, :channels], table_ref[:, lanes])

    @pl.when(step >= 2 * blocks)
    def _():
        lanes = pl.ds(pl.multiple_of((step - 2 * blocks) * WIDE, WIDE), WIDE)
        rows = residual_ref[:, lanes].astype(jnp.float32)
        out_ref[...] = (rows + product(held_ref[...], first_ref[...])).astype(jnp.bfloat16)


def hidden_kernel(values_ref, center_ref, scale_ref, order_ref, out_ref, held_ref, table_ref):
    scaled = (values_ref[...].astype(jnp.float32) - center_ref[...]) * scale_ref[...]
    held_ref[...] = jax.nn.silu(scaled).astype(jnp.bfloat16)

    @pl.loop(0, held_ref.shape[1] // WIDE)
    def _(part):
        lanes = pl.ds(pl.multiple_of(part * WIDE, WIDE), WIDE)
        order = order_ref[:, lanes]
        channel = lax.broadcasted_iota(jnp.int32, table_ref.shape, 0)
        table_ref[...] = (channel == order).astype(jnp.bfloat16)
        out_ref[:, lanes] = moved(held_ref[...], table_ref[...])


def hidden_of(values, center, scale, order):
    return pl.pallas_call(
        hidden_kernel,
        out_shape=jax.ShapeDtypeStruct(values.shape, jnp.bfloat16),
        scratch_shapes=[
            pltpu.VMEM(values.shape, jnp.bfloat16),
            pltpu.VMEM((values.shape[1], WIDE), jnp.bfloat16),
        ],
        cost_estimate=pl.CostEstimate(
            flops=2 * values.shape[0] * values.shape[1] ** 2,
            bytes_accessed=4 * values.size,
            transcendentals=values.size,
        ),
    )(values, center, scale, order)


def block(hidden, values, bias, order, attend_order, weights, attend_weights):
    count, channels = hidden.shape
    blocks = channels // WIDE
    whole = lambda array: pl.BlockSpec(array.shape, lambda i: (0, 0))

    def weight(part):
        def at(i):
            tail = i + blocks if part == 0 else part * blocks + blocks - 1
            early = jnp.minimum(i, blocks - 1) + part * blocks
            return 0, jnp.where(i < 2 * blocks, early, tail)

        return pl.BlockSpec((channels, WIDE), at)

    def attend_weight(depth, which):
        at = lambda i: (0, jnp.clip(i - blocks, 0, blocks - 1) + which * blocks)
        return pl.BlockSpec((depth, WIDE), at)

    return pl.pallas_call(
        block_kernel,
        grid=(3 * blocks,),
        in_specs=[whole(array) for array in (hidden, values, bias, order, attend_order)]
        + [weight(part) for part in range(3)]
        + [attend_weight(depth, which) for _, depth in PARTS for which in range(3)],
        out_specs=pl.BlockSpec((count, WIDE), lambda i: (0, jnp.maximum(i - 2 * blocks, 0))),
        out_shape=jax.ShapeDtypeStruct((count, channels), jnp.bfloat16),
        scratch_shapes=[
            pltpu.VMEM((channels, channels), jnp.bfloat16),
            pltpu.VMEM((channels, PADDED), jnp.bfloat16),
            pltpu.VMEM((count, channels), jnp.bfloat16),
            pltpu.VMEM((count, PADDED), jnp.bfloat16),
            pltpu.VMEM((count, channels), jnp.bfloat16),
            pltpu.VMEM((count, channels), jnp.bfloat16),
        ],
        cost_estimate=pl.CostEstimate(
            flops=2 * count * channels * 9 * channels,
            bytes_accessed=14 * channels * channels + 8 * count * channels,
            transcendentals=count * count * HEADS // 2,
        ),
    )(
        hidden, values, bias, order, attend_order, weights, weights, weights,
        *[array for array in attend_weights for _ in range(3)]
    )


def shards(latents, timestep, norm_gain, time_weight, conv_weight, attend_weight, output_weight):
    _, frames_dev, pixels, channels = latents.shape
    my = {axis: lax.axis_index(axis) for axis in ALL}
    frame = my["x"] * 4 + my["y"]

    piece = jnp.concatenate(
        [conv_weight[t] for t in range(3)]
        + [
            output_weight,
            lax.dynamic_index_in_dim(time_weight.reshape(20, 16, 80), frame, 1, False).reshape(5, 320),
        ],
        axis=1,
    ).reshape(-1)
    near = [shifted(piece, "z", step) for step in RING[1:5]]
    flat = attend_weight.reshape(-1)
    line = [flat] + [shifted(flat, "y", step) for step in SMALL[1:]]
    near, line = lax.optimization_barrier((near, line))
    far = [shifted(near[2], "z", 1), shifted(near[3], "z", -1), shifted(near[2], "z", 2)]
    line = jnp.concatenate(line)
    plane = [line] + [shifted(line, "x", step) for step in SMALL[1:]]
    square = jnp.stack(plane).reshape(80, 3 * channels)
    stage = jnp.stack([piece] + near + far).reshape(8, 5, -1)
    mixing = stage[:, :, : 4 * channels].reshape(40, 4 * channels)
    mixing = lax.all_gather(mixing, ("core", "x", "y"), axis=0, tiled=True)

    back, ahead = shifted(square, "z", 1), shifted(square, "z", -1)
    latents, stage, back, ahead = lax.optimization_barrier((latents, stage, back, ahead))
    chunks = [square, back, ahead]
    for _ in range(2):
        back, ahead = shifted(back, "z", 1), shifted(ahead, "z", -1)
        chunks += [back, ahead]
    chunks.append(shifted(back, "z", 1))
    own = [jnp.concatenate(chunks, axis=0)]
    attending = own + [shifted(part, "core", 1) for part in own]

    values = lax.all_to_all(latents, FRAME, split_axis=2, concat_axis=1, tiled=True)
    values = values.reshape(-1, channels)

    here = latents.reshape(-1, channels).astype(jnp.float32)
    width = channels // GROUPS
    members = here.shape[0] * width
    mean_here = jnp.sum(jnp.sum(here, axis=0).reshape(GROUPS, width), axis=1) / members
    deviate = here - jnp.repeat(mean_here, width)[None, :]
    square_here = jnp.sum(jnp.sum(deviate * deviate, axis=0).reshape(GROUPS, width), axis=1)
    features = sinusoid(timestep).astype(jnp.bfloat16).reshape(8, 2, 20)
    features = features[(my["z"] - jnp.asarray(RING)) % 8]
    time_rows = stage[:, :, 4 * channels :].reshape(160, 80)
    time_other = shifted(time_rows, "core", 1)
    bias_here = jnp.zeros((1, 80), jnp.float32)
    for core, rows in ((my["core"], time_rows), (1 - my["core"], time_other)):
        part = lax.dynamic_index_in_dim(features, core, 1, False).reshape(1, 160)
        bias_here = bias_here + jnp.dot(part, rows, preferred_element_type=jnp.float32)
    sums = jnp.concatenate([mean_here, square_here, bias_here[0]])[None, :]
    sums = lax.all_to_all(jnp.broadcast_to(sums[None], (16, *sums.shape)), FRAME, 0, 0, tiled=True)
    sums = sums.reshape(16, -1)
    means, squares = sums[:, :GROUPS], sums[:, GROUPS : 2 * GROUPS]
    time_bias = sums[:, 2 * GROUPS :].reshape(1, channels)
    center = jnp.mean(means, axis=0)
    spread = jnp.sum(squares, axis=0) + members * jnp.sum((means - center) ** 2, axis=0)
    spread = spread / (16 * members)
    scale = norm_gain / jnp.sqrt(jnp.repeat(spread, width) + 1e-05)

    ring, small = np.array(RING), np.array(SMALL)
    core, x, y, z, row = np.indices((2, 4, 4, 8, 5)).reshape(5, -1)
    order = channel_of((my["z"] - ring[z]) % 8, core, x, y, row)
    part, z, x, y, row = np.indices((2, 8, 4, 4, 5)).reshape(5, -1)
    core = jnp.where(part == 0, my["core"], 1 - my["core"])
    places = [(my["z"] - ring[z]) % 8, core, (my["x"] - small[x]) % 4, (my["y"] - small[y]) % 4]
    attend_order = channel_of(*places, row)
    spaced, begin = [], 0
    for (at, depth), end in zip(PARTS, [at for at, _ in PARTS[1:]] + [PADDED]):
        spaced += [attend_order[begin : begin + depth], jnp.full(end - at - depth, -1)]
        begin += depth
    attend_order = jnp.concatenate(spaced)

    center = jnp.repeat(center, width)[None, :]
    hidden = hidden_of(values, center, scale[None, :], order[None, :])
    mixed = block(
        hidden, values, time_bias, order[None, :], attend_order[None, :], mixing, attending
    )
    mixed = mixed.reshape(1, -1, 8, channels)
    return lax.all_to_all(mixed, FRAME, split_axis=1, concat_axis=2, tiled=True)


def solution(mesh):
    split = Mesh(mesh.devices.reshape(8, 2, 4, 4), ALL)
    placed = (
        P(DP, FRAME, None, None),
        P(DP),
        P(),
        P(DP, None),
        P(None, ALL, None),
        P(ALL, None),
        P(ALL, None),
    )
    return jax.shard_map(
        shards, mesh=split, in_specs=placed, out_specs=P(DP, FRAME, None, None), check_vma=False
    )
```

```python
import math

import jax
import jax.numpy as jnp
import numpy as np
from jax import lax
from jax.experimental import pallas as pl
from jax.experimental.pallas import tpu as pltpu
from jax.sharding import Mesh
from jax.sharding import PartitionSpec as P


HEADS = 20
HD = 64
GROUPS = 32
TEMB = 320
FRAME = ("x", "y")
DP = ("z", "core")
ALL = ("z", "core", "x", "y")


def shifted(array, axis, step):
    count = lax.axis_size(axis)
    return lax.ppermute(array, axis, [(i, (i + step) % count) for i in range(count)])


RING = (0, 1, -1, 2, -2, 3, -3, 4)
SMALL = (0, 1, -1, 2)


def channel_of(z, core, x, y, row):
    return z * 160 + core * 80 + x * 20 + y * 5 + row


def moved(array, table):
    return jnp.dot(array, table, preferred_element_type=jnp.float32).astype(jnp.bfloat16)


def sinusoid(timestep):
    half_dim = TEMB // 2
    ladder = jnp.arange(half_dim, dtype=jnp.float32)
    freqs = jnp.exp(-math.log(10000.0) * ladder / half_dim)
    angles = timestep.astype(jnp.float32)[:, None] * freqs[None, :]
    return jnp.concatenate([jnp.cos(angles), jnp.sin(angles)], axis=-1)


def attended_pair(query, key, value, first, same):
    results = []
    for mine in (first, jnp.logical_not(first)):
        part = jnp.where(mine, query, jnp.zeros_like(query)) * (1.0 / math.sqrt(HD))
        scores = lax.dot_general(
            part.astype(jnp.bfloat16),
            key,
            (((1,), (1,)), ((), ())),
            preferred_element_type=jnp.float32,
        )
        scores = jnp.where(same, scores, -3e38)
        expo = jnp.exp(scores - jnp.max(scores, axis=-1, keepdims=True)).astype(jnp.bfloat16)
        padded = jnp.where(mine, value, jnp.ones_like(value))
        results.append(jnp.dot(expo, padded, preferred_element_type=jnp.float32))
    sums = pltpu.roll(jnp.where(first, results[1], results[0]), HD, 1)
    return (jnp.where(first, results[0], results[1]) / sums).astype(jnp.bfloat16)


WIDE = 256
PADDED = 1536
PARTS = ((0, 640), (768, 640))


def fill(table_ref, order_ref, lanes):
    order = order_ref[:, lanes]
    channel = lax.broadcasted_iota(jnp.int32, (table_ref.shape[0], order.shape[1]), 0)
    table_ref[:, lanes] = (channel == order).astype(jnp.bfloat16)


def conv_kernel(
    hidden_ref, values_ref, bias_ref, order_ref, first_ref, middle_ref, last_ref,
    residual_ref, mixed_ref, table_ref, held_ref
):
    count, channels = hidden_ref.shape
    frames = count // 8
    blocks = channels // WIDE
    step = pl.program_id(0)
    lanes = pl.ds(pl.multiple_of(step * WIDE, WIDE), WIDE)
    fill(table_ref, order_ref, lanes)

    @pl.when(step < blocks)
    def _():
        hidden = hidden_ref[...]
        first, middle, last = [
            jnp.dot(hidden, ref[...], preferred_element_type=jnp.float32)
            for ref in (first_ref, middle_ref, last_ref)
        ]
        edge = jnp.zeros((8, WIDE), jnp.float32)
        before = jnp.concatenate([edge, first[:-8]], axis=0)
        after = jnp.concatenate([last[8:], edge], axis=0)
        conv = before + middle + after + bias_ref[:, lanes]
        residual_ref[:, lanes] = (values_ref[:, lanes].astype(jnp.float32) + conv).astype(
            jnp.bfloat16
        )

    @pl.when(step == blocks)
    def _():
        to = lax.broadcasted_iota(jnp.int32, (count, count), 0)
        source = lax.broadcasted_iota(jnp.int32, (count, count), 1)
        rows = residual_ref[...].astype(jnp.float32)
        centered = rows - jnp.mean(rows, axis=-1, keepdims=True)
        variance = jnp.mean(centered * centered, axis=-1, keepdims=True)
        normed = (centered / jnp.sqrt(variance + 1e-05)).astype(jnp.bfloat16)
        by_pixel = (source == (to % frames) * 8 + to // frames).astype(jnp.bfloat16)
        held_ref[...] = moved(by_pixel, normed)

        @pl.loop(0, PADDED // WIDE)
        def _(part):
            lanes = pl.ds(pl.multiple_of(part * WIDE, WIDE), WIDE)
            mixed_ref[:, lanes] = moved(held_ref[...], table_ref[:, lanes])


def convolve(hidden, values, bias, order, weights):
    count, channels = hidden.shape
    blocks = channels // WIDE
    whole = lambda array: pl.BlockSpec(array.shape, lambda i: (0, 0))
    weight = lambda tap: pl.BlockSpec(
        (channels, WIDE), lambda i: (0, jnp.minimum(i, blocks - 1) + tap * blocks)
    )
    shapes = [jax.ShapeDtypeStruct((count, w), jnp.bfloat16) for w in (channels, PADDED)]
    return pl.pallas_call(
        conv_kernel,
        grid=(PADDED // WIDE,),
        in_specs=[whole(array) for array in (hidden, values, bias, order)]
        + [weight(tap) for tap in range(3)],
        out_specs=[whole(shape) for shape in shapes],
        out_shape=shapes,
        scratch_shapes=[
            pltpu.VMEM((channels, PADDED), jnp.bfloat16),
            pltpu.VMEM((count, channels), jnp.bfloat16),
        ],
        cost_estimate=pl.CostEstimate(
            flops=2 * count * channels * 4 * channels,
            bytes_accessed=6 * channels * channels + 10 * count * channels,
            transcendentals=0,
        ),
    )(hidden, values, bias, order, weights, weights, weights)


def attend_kernel(mixed_ref, residual_ref, order_ref, *refs):
    attend_refs, refs = refs[: 3 * len(PARTS)], refs[3 * len(PARTS) :]
    output_ref, out_ref, table_ref, held_ref, attended_ref = refs
    count, channels = residual_ref.shape
    frames = count // 8
    blocks = channels // WIDE
    step = pl.program_id(0)
    product = lambda left, right: jnp.dot(left, right, preferred_element_type=jnp.float32)

    @pl.when(step < blocks)
    def _():
        triple = []
        for which in range(3):
            total = 0.0
            for part, (at, depth) in enumerate(PARTS):
                weight = attend_refs[part * 3 + which][...]
                total = total + product(mixed_ref[:, at : at + depth], weight)
            triple.append(total.astype(jnp.bfloat16))
        query, key, value = triple
        group = count // 2
        first = lax.broadcasted_iota(jnp.int32, (group, 128), 1) < HD
        same = (
            lax.broadcasted_iota(jnp.int32, (group, group), 0) // frames
            == lax.broadcasted_iota(jnp.int32, (group, group), 1) // frames
        )
        base = step * WIDE
        for place in range(2):
            cut = slice(place * group, (place + 1) * group)
            for pair in range(WIDE // 128):
                lanes = slice(pair * 128, (pair + 1) * 128)
                target = pl.ds(pl.multiple_of(base + pair * 128, 128), 128)
                attended_ref[cut, target] = attended_pair(
                    query[cut, lanes], key[cut, lanes], value[cut, lanes], first, same
                )
        fill(table_ref, order_ref, pl.ds(pl.multiple_of(base, WIDE), WIDE))

    @pl.when(step == blocks)
    def _():
        to = lax.broadcasted_iota(jnp.int32, (count, count), 0)
        source = lax.broadcasted_iota(jnp.int32, (count, count), 1)
        by_frame = (source == (to % 8) * frames + to // 8).astype(jnp.bfloat16)
        attended_ref[...] = moved(by_frame, attended_ref[...])

        @pl.loop(0, blocks)
        def _(part):
            lanes = pl.ds(pl.multiple_of(part * WIDE, WIDE), WIDE)
            held_ref[:, lanes] = moved(attended_ref[...], table_ref[:, lanes])

    @pl.when(step >= blocks)
    def _():
        lanes = pl.ds(pl.multiple_of((step - blocks) * WIDE, WIDE), WIDE)
        rows = residual_ref[:, lanes].astype(jnp.float32)
        out_ref[...] = (rows + product(held_ref[...], output_ref[...])).astype(jnp.bfloat16)


def attend(mixed, residual, order, attend_weights, weights):
    count, channels = residual.shape
    blocks = channels // WIDE
    whole = lambda array: pl.BlockSpec(array.shape, lambda i: (0, 0))
    late = lambda i: jnp.maximum(i - blocks, 0)

    def attend_weight(depth, which):
        at = lambda i: (0, jnp.minimum(i, blocks - 1) + which * blocks)
        return pl.BlockSpec((depth, WIDE), at)

    return pl.pallas_call(
        attend_kernel,
        grid=(2 * blocks,),
        in_specs=[whole(array) for array in (mixed, residual, order)]
        + [attend_weight(depth, which) for _, depth in PARTS for which in range(3)]
        + [pl.BlockSpec((channels, WIDE), lambda i: (0, late(i) + 3 * blocks))],
        out_specs=pl.BlockSpec((count, WIDE), lambda i: (0, late(i))),
        out_shape=jax.ShapeDtypeStruct((count, channels), jnp.bfloat16),
        scratch_shapes=[
            pltpu.VMEM((channels, channels), jnp.bfloat16),
            pltpu.VMEM((count, channels), jnp.bfloat16),
            pltpu.VMEM((count, channels), jnp.bfloat16),
        ],
        cost_estimate=pl.CostEstimate(
            flops=2 * count * channels * 5 * channels,
            bytes_accessed=8 * channels * channels + 8 * count * channels,
            transcendentals=count * count * HEADS // 2,
        ),
    )(mixed, residual, order, *[a for a in attend_weights for _ in range(3)], weights)


def hidden_kernel(values_ref, center_ref, scale_ref, order_ref, out_ref, held_ref, table_ref):
    scaled = (values_ref[...].astype(jnp.float32) - center_ref[...]) * scale_ref[...]
    held_ref[...] = jax.nn.silu(scaled).astype(jnp.bfloat16)

    @pl.loop(0, held_ref.shape[1] // WIDE)
    def _(part):
        lanes = pl.ds(pl.multiple_of(part * WIDE, WIDE), WIDE)
        order = order_ref[:, lanes]
        channel = lax.broadcasted_iota(jnp.int32, table_ref.shape, 0)
        table_ref[...] = (channel == order).astype(jnp.bfloat16)
        out_ref[:, lanes] = moved(held_ref[...], table_ref[...])


def hidden_of(values, center, scale, order):
    return pl.pallas_call(
        hidden_kernel,
        out_shape=jax.ShapeDtypeStruct(values.shape, jnp.bfloat16),
        scratch_shapes=[
            pltpu.VMEM(values.shape, jnp.bfloat16),
            pltpu.VMEM((values.shape[1], WIDE), jnp.bfloat16),
        ],
        cost_estimate=pl.CostEstimate(
            flops=2 * values.shape[0] * values.shape[1] ** 2,
            bytes_accessed=4 * values.size,
            transcendentals=values.size,
        ),
    )(values, center, scale, order)


def block(hidden, values, bias, order, attend_order, weights, attend_weights):
    count, channels = hidden.shape
    blocks = channels // WIDE
    whole = lambda array: pl.BlockSpec(array.shape, lambda i: (0, 0))

    def weight(part):
        def at(i):
            tail = i + blocks if part == 0 else part * blocks + blocks - 1
            early = jnp.minimum(i, blocks - 1) + part * blocks
            return 0, jnp.where(i < 2 * blocks, early, tail)

        return pl.BlockSpec((channels, WIDE), at)

    def attend_weight(depth, which):
        at = lambda i: (0, jnp.clip(i - blocks, 0, blocks - 1) + which * blocks)
        return pl.BlockSpec((depth, WIDE), at)

    return pl.pallas_call(
        block_kernel,
        grid=(3 * blocks,),
        in_specs=[whole(array) for array in (hidden, values, bias, order, attend_order)]
        + [weight(part) for part in range(3)]
        + [attend_weight(depth, which) for _, depth in PARTS for which in range(3)],
        out_specs=pl.BlockSpec((count, WIDE), lambda i: (0, jnp.maximum(i - 2 * blocks, 0))),
        out_shape=jax.ShapeDtypeStruct((count, channels), jnp.bfloat16),
        scratch_shapes=[
            pltpu.VMEM((channels, channels), jnp.bfloat16),
            pltpu.VMEM((channels, PADDED), jnp.bfloat16),
            pltpu.VMEM((count, channels), jnp.bfloat16),
            pltpu.VMEM((count, PADDED), jnp.bfloat16),
            pltpu.VMEM((count, channels), jnp.bfloat16),
            pltpu.VMEM((count, channels), jnp.bfloat16),
        ],
        cost_estimate=pl.CostEstimate(
            flops=2 * count * channels * 9 * channels,
            bytes_accessed=14 * channels * channels + 8 * count * channels,
            transcendentals=count * count * HEADS // 2,
        ),
    )(
        hidden, values, bias, order, attend_order, weights, weights, weights,
        *[array for array in attend_weights for _ in range(3)]
    )


def shards(latents, timestep, norm_gain, time_weight, conv_weight, attend_weight, output_weight):
    _, frames_dev, pixels, channels = latents.shape
    my = {axis: lax.axis_index(axis) for axis in ALL}
    frame = my["x"] * 4 + my["y"]

    piece = jnp.concatenate(
        [conv_weight[t] for t in range(3)]
        + [
            output_weight,
            lax.dynamic_index_in_dim(time_weight.reshape(20, 16, 80), frame, 1, False).reshape(5, 320),
        ],
        axis=1,
    ).reshape(-1)
    near = [shifted(piece, "z", step) for step in RING[1:5]]
    flat = attend_weight.reshape(-1)
    line = [flat] + [shifted(flat, "y", step) for step in SMALL[1:]]
    near, line = lax.optimization_barrier((near, line))
    far = [shifted(near[2], "z", 1), shifted(near[3], "z", -1), shifted(near[2], "z", 2)]
    line = jnp.concatenate(line)
    plane = [line] + [shifted(line, "x", step) for step in SMALL[1:]]
    square = jnp.stack(plane).reshape(80, 3 * channels)
    stage = jnp.stack([piece] + near + far).reshape(8, 5, -1)
    mixing = stage[:, :, : 4 * channels].reshape(40, 4 * channels)
    mixing = lax.all_gather(mixing, ("core", "x", "y"), axis=0, tiled=True)

    latents, stage, square = lax.optimization_barrier((latents, stage, square))
    back, ahead = shifted(square, "z", 1), shifted(square, "z", -1)
    chunks = [square, back, ahead]

    here = latents.reshape(-1, channels).astype(jnp.float32)
    width = channels // GROUPS
    members = here.shape[0] * width
    mean_here = jnp.sum(jnp.sum(here, axis=0).reshape(GROUPS, width), axis=1) / members
    deviate = here - jnp.repeat(mean_here, width)[None, :]
    square_here = jnp.sum(jnp.sum(deviate * deviate, axis=0).reshape(GROUPS, width), axis=1)
    features = sinusoid(timestep).astype(jnp.bfloat16).reshape(8, 2, 20)
    features = features[(my["z"] - jnp.asarray(RING)) % 8]
    time_rows = stage[:, :, 4 * channels :].reshape(160, 80)
    time_other = shifted(time_rows, "core", 1)
    bias_here = jnp.zeros((1, 80), jnp.float32)
    for core, rows in ((my["core"], time_rows), (1 - my["core"], time_other)):
        part = lax.dynamic_index_in_dim(features, core, 1, False).reshape(1, 160)
        bias_here = bias_here + jnp.dot(part, rows, preferred_element_type=jnp.float32)
    sums = jnp.concatenate([mean_here, square_here, bias_here[0]])[None, :]
    back, ahead, sums = lax.optimization_barrier((back, ahead, sums))

    back, ahead = shifted(back, "z", 1), shifted(ahead, "z", -1)
    chunks += [back, ahead]
    sums = lax.all_to_all(jnp.broadcast_to(sums[None], (16, *sums.shape)), FRAME, 0, 0, tiled=True)
    back, ahead, sums = lax.optimization_barrier((back, ahead, sums))

    back, ahead = shifted(back, "z", 1), shifted(ahead, "z", -1)
    chunks += [back, ahead]
    latents, _ = lax.optimization_barrier((latents, sums))
    values = lax.all_to_all(latents, FRAME, split_axis=2, concat_axis=1, tiled=True)
    back, values = lax.optimization_barrier((back, values))
    chunks.append(shifted(back, "z", 1))
    values = values.reshape(-1, channels)
    sums = sums.reshape(16, -1)
    means, squares = sums[:, :GROUPS], sums[:, GROUPS : 2 * GROUPS]
    time_bias = sums[:, 2 * GROUPS :].reshape(1, channels)
    center = jnp.mean(means, axis=0)
    spread = jnp.sum(squares, axis=0) + members * jnp.sum((means - center) ** 2, axis=0)
    spread = spread / (16 * members)
    scale = norm_gain / jnp.sqrt(jnp.repeat(spread, width) + 1e-05)

    ring, small = np.array(RING), np.array(SMALL)
    core, x, y, z, row = np.indices((2, 4, 4, 8, 5)).reshape(5, -1)
    order = channel_of((my["z"] - ring[z]) % 8, core, x, y, row)
    part, z, x, y, row = np.indices((2, 8, 4, 4, 5)).reshape(5, -1)
    core = jnp.where(part == 0, my["core"], 1 - my["core"])
    places = [(my["z"] - ring[z]) % 8, core, (my["x"] - small[x]) % 4, (my["y"] - small[y]) % 4]
    attend_order = channel_of(*places, row)
    spaced, begin = [], 0
    for (at, depth), end in zip(PARTS, [at for at, _ in PARTS[1:]] + [PADDED]):
        spaced += [attend_order[begin : begin + depth], jnp.full(end - at - depth, -1)]
        begin += depth
    attend_order = jnp.concatenate(spaced)

    center = jnp.repeat(center, width)[None, :]
    hidden = hidden_of(values, center, scale[None, :], order[None, :])
    own = jnp.concatenate(chunks, axis=0)
    own, mixing = lax.optimization_barrier((own, mixing))
    attending = [own, shifted(own, "core", 1)]
    residual, mixed = convolve(hidden, values, time_bias, attend_order[None, :], mixing)
    mixed = attend(mixed, residual, order[None, :], attending, mixing)
    mixed = mixed.reshape(1, -1, 8, channels)
    return lax.all_to_all(mixed, FRAME, split_axis=1, concat_axis=2, tiled=True)


def solution(mesh):
    split = Mesh(mesh.devices.reshape(8, 2, 4, 4), ALL)
    placed = (
        P(DP, FRAME, None, None),
        P(DP),
        P(),
        P(DP, None),
        P(None, ALL, None),
        P(ALL, None),
        P(ALL, None),
    )
    return jax.shard_map(
        shards, mesh=split, in_specs=placed, out_specs=P(DP, FRAME, None, None), check_vma=False
    )
```

```python
import math

import jax
import jax.numpy as jnp
import numpy as np
from jax import lax
from jax.experimental import pallas as pl
from jax.experimental.pallas import tpu as pltpu
from jax.sharding import Mesh
from jax.sharding import PartitionSpec as P


HEADS = 20
HD = 64
GROUPS = 32
TEMB = 320
FRAME = ("x", "y")
DP = ("z", "core")
ALL = ("z", "core", "x", "y")


def shifted(array, axis, step):
    count = lax.axis_size(axis)
    return lax.ppermute(array, axis, [(i, (i + step) % count) for i in range(count)])


RING = (0, 1, -1, 2, -2, 3, -3, 4)
SMALL = (0, 1, -1, 2)


def channel_of(z, core, x, y, row):
    return z * 160 + core * 80 + x * 20 + y * 5 + row


def moved(array, table):
    return jnp.dot(array, table, preferred_element_type=jnp.float32).astype(jnp.bfloat16)


def sinusoid(timestep):
    half_dim = TEMB // 2
    ladder = jnp.arange(half_dim, dtype=jnp.float32)
    freqs = jnp.exp(-math.log(10000.0) * ladder / half_dim)
    angles = timestep.astype(jnp.float32)[:, None] * freqs[None, :]
    return jnp.concatenate([jnp.cos(angles), jnp.sin(angles)], axis=-1)


def attended_pair(query, key, value, first, same):
    results = []
    for mine in (first, jnp.logical_not(first)):
        part = jnp.where(mine, query, jnp.zeros_like(query)) * (1.0 / math.sqrt(HD))
        scores = lax.dot_general(
            part.astype(jnp.bfloat16),
            key,
            (((1,), (1,)), ((), ())),
            preferred_element_type=jnp.float32,
        )
        scores = jnp.where(same, scores, -3e38)
        expo = jnp.exp(scores - jnp.max(scores, axis=-1, keepdims=True)).astype(jnp.bfloat16)
        padded = jnp.where(mine, value, jnp.ones_like(value))
        results.append(jnp.dot(expo, padded, preferred_element_type=jnp.float32))
    sums = pltpu.roll(jnp.where(first, results[1], results[0]), HD, 1)
    return (jnp.where(first, results[0], results[1]) / sums).astype(jnp.bfloat16)


WIDE = 256
PADDED = 1280
PARTS = (640, 640)


def fill(table_ref, order_ref, lanes):
    order = order_ref[:, lanes]
    channel = lax.broadcasted_iota(jnp.int32, (table_ref.shape[0], order.shape[1]), 0)
    table_ref[:, lanes] = (channel == order).astype(jnp.bfloat16)


def conv_kernel(
    hidden_ref, values_ref, bias_ref, order_ref, first_ref, middle_ref, last_ref,
    residual_ref, mixed_ref, table_ref, held_ref
):
    count, channels = hidden_ref.shape
    frames = count // 8
    blocks = channels // WIDE
    step = pl.program_id(0)
    @pl.when(step < blocks)
    def _():
        lanes = pl.ds(pl.multiple_of(step * WIDE, WIDE), WIDE)
        fill(table_ref, order_ref, lanes)
        hidden = hidden_ref[...]
        first, middle, last = [
            jnp.dot(hidden, ref[...], preferred_element_type=jnp.float32)
            for ref in (first_ref, middle_ref, last_ref)
        ]
        edge = jnp.zeros((8, WIDE), jnp.float32)
        before = jnp.concatenate([edge, first[:-8]], axis=0)
        after = jnp.concatenate([last[8:], edge], axis=0)
        conv = before + middle + after + bias_ref[:, lanes]
        residual_ref[:, lanes] = (values_ref[:, lanes].astype(jnp.float32) + conv).astype(
            jnp.bfloat16
        )

    @pl.when(step == blocks)
    def _():
        to = lax.broadcasted_iota(jnp.int32, (count, count), 0)
        source = lax.broadcasted_iota(jnp.int32, (count, count), 1)
        rows = residual_ref[...].astype(jnp.float32)
        centered = rows - jnp.mean(rows, axis=-1, keepdims=True)
        variance = jnp.mean(centered * centered, axis=-1, keepdims=True)
        normed = (centered / jnp.sqrt(variance + 1e-05)).astype(jnp.bfloat16)
        by_pixel = (source == (to % frames) * 8 + to // frames).astype(jnp.bfloat16)
        held_ref[...] = moved(by_pixel, normed)

        @pl.loop(0, PADDED // WIDE)
        def _(part):
            lanes = pl.ds(pl.multiple_of(part * WIDE, WIDE), WIDE)
            mixed_ref[:, lanes] = moved(held_ref[...], table_ref[:, lanes])


def convolve(hidden, values, bias, order, weights):
    count, channels = hidden.shape
    blocks = channels // WIDE
    whole = lambda array: pl.BlockSpec(array.shape, lambda i: (0, 0))
    weight = lambda tap: pl.BlockSpec(
        (channels, WIDE), lambda i: (0, jnp.minimum(i, blocks - 1) + tap * blocks)
    )
    shapes = [jax.ShapeDtypeStruct((count, w), jnp.bfloat16) for w in (channels, PADDED)]
    return pl.pallas_call(
        conv_kernel,
        grid=(blocks + 1,),
        in_specs=[whole(array) for array in (hidden, values, bias, order)]
        + [weight(tap) for tap in range(3)],
        out_specs=[whole(shape) for shape in shapes],
        out_shape=shapes,
        scratch_shapes=[
            pltpu.VMEM((channels, PADDED), jnp.bfloat16),
            pltpu.VMEM((count, channels), jnp.bfloat16),
        ],
        cost_estimate=pl.CostEstimate(
            flops=2 * count * channels * 4 * channels,
            bytes_accessed=6 * channels * channels + 10 * count * channels,
            transcendentals=0,
        ),
    )(hidden, values, bias, order, weights, weights, weights)


def attend_kernel(mixed_ref, residual_ref, order_ref, *refs):
    attend_refs, refs = refs[: 3 * len(PARTS)], refs[3 * len(PARTS) :]
    output_ref, out_ref, table_ref, held_ref, attended_ref = refs
    count, channels = residual_ref.shape
    frames = count // 8
    blocks = channels // WIDE
    step = pl.program_id(0)
    product = lambda left, right: jnp.dot(left, right, preferred_element_type=jnp.float32)

    @pl.when(step < blocks)
    def _():
        triple = []
        for which in range(3):
            weight = [attend_refs[part * 3 + which][...] for part in range(len(PARTS))]
            weight = jnp.concatenate(weight, axis=0)
            triple.append(product(mixed_ref[...], weight).astype(jnp.bfloat16))
        query, key, value = triple
        group = count // 2
        first = lax.broadcasted_iota(jnp.int32, (group, 128), 1) < HD
        same = (
            lax.broadcasted_iota(jnp.int32, (group, group), 0) // frames
            == lax.broadcasted_iota(jnp.int32, (group, group), 1) // frames
        )
        base = step * WIDE
        for place in range(2):
            cut = slice(place * group, (place + 1) * group)
            for pair in range(WIDE // 128):
                lanes = slice(pair * 128, (pair + 1) * 128)
                target = pl.ds(pl.multiple_of(base + pair * 128, 128), 128)
                attended_ref[cut, target] = attended_pair(
                    query[cut, lanes], key[cut, lanes], value[cut, lanes], first, same
                )
        fill(table_ref, order_ref, pl.ds(pl.multiple_of(base, WIDE), WIDE))

    @pl.when(step == blocks)
    def _():
        to = lax.broadcasted_iota(jnp.int32, (count, count), 0)
        source = lax.broadcasted_iota(jnp.int32, (count, count), 1)
        by_frame = (source == (to % 8) * frames + to // 8).astype(jnp.bfloat16)
        attended_ref[...] = moved(by_frame, attended_ref[...])

        @pl.loop(0, blocks)
        def _(part):
            lanes = pl.ds(pl.multiple_of(part * WIDE, WIDE), WIDE)
            held_ref[:, lanes] = moved(attended_ref[...], table_ref[:, lanes])

    @pl.when(step >= blocks)
    def _():
        lanes = pl.ds(pl.multiple_of((step - blocks) * WIDE, WIDE), WIDE)
        rows = residual_ref[:, lanes].astype(jnp.float32)
        out_ref[...] = (rows + product(held_ref[...], output_ref[...])).astype(jnp.bfloat16)


def attend(mixed, residual, order, attend_weights, weights):
    count, channels = residual.shape
    blocks = channels // WIDE
    whole = lambda array: pl.BlockSpec(array.shape, lambda i: (0, 0))
    late = lambda i: jnp.maximum(i - blocks, 0)

    def attend_weight(depth, which):
        at = lambda i: (0, jnp.minimum(i, blocks - 1) + which * blocks)
        return pl.BlockSpec((depth, WIDE), at)

    return pl.pallas_call(
        attend_kernel,
        grid=(2 * blocks,),
        in_specs=[whole(array) for array in (mixed, residual, order)]
        + [attend_weight(depth, which) for depth in PARTS for which in range(3)]
        + [pl.BlockSpec((channels, WIDE), lambda i: (0, late(i) + 3 * blocks))],
        out_specs=pl.BlockSpec((count, WIDE), lambda i: (0, late(i))),
        out_shape=jax.ShapeDtypeStruct((count, channels), jnp.bfloat16),
        scratch_shapes=[
            pltpu.VMEM((channels, channels), jnp.bfloat16),
            pltpu.VMEM((count, channels), jnp.bfloat16),
            pltpu.VMEM((count, channels), jnp.bfloat16),
        ],
        cost_estimate=pl.CostEstimate(
            flops=2 * count * channels * 5 * channels,
            bytes_accessed=8 * channels * channels + 8 * count * channels,
            transcendentals=count * count * HEADS // 2,
        ),
    )(mixed, residual, order, *[a for a in attend_weights for _ in range(3)], weights)


def hidden_kernel(values_ref, center_ref, scale_ref, order_ref, out_ref, held_ref, table_ref):
    scaled = (values_ref[...].astype(jnp.float32) - center_ref[...]) * scale_ref[...]
    held_ref[...] = jax.nn.silu(scaled).astype(jnp.bfloat16)

    @pl.loop(0, held_ref.shape[1] // WIDE)
    def _(part):
        lanes = pl.ds(pl.multiple_of(part * WIDE, WIDE), WIDE)
        order = order_ref[:, lanes]
        channel = lax.broadcasted_iota(jnp.int32, table_ref.shape, 0)
        table_ref[...] = (channel == order).astype(jnp.bfloat16)
        out_ref[:, lanes] = moved(held_ref[...], table_ref[...])


def hidden_of(values, center, scale, order):
    return pl.pallas_call(
        hidden_kernel,
        out_shape=jax.ShapeDtypeStruct(values.shape, jnp.bfloat16),
        scratch_shapes=[
            pltpu.VMEM(values.shape, jnp.bfloat16),
            pltpu.VMEM((values.shape[1], WIDE), jnp.bfloat16),
        ],
        cost_estimate=pl.CostEstimate(
            flops=2 * values.shape[0] * values.shape[1] ** 2,
            bytes_accessed=4 * values.size,
            transcendentals=values.size,
        ),
    )(values, center, scale, order)


def block(hidden, values, bias, order, attend_order, weights, attend_weights):
    count, channels = hidden.shape
    blocks = channels // WIDE
    whole = lambda array: pl.BlockSpec(array.shape, lambda i: (0, 0))

    def weight(part):
        def at(i):
            tail = i + blocks if part == 0 else part * blocks + blocks - 1
            early = jnp.minimum(i, blocks - 1) + part * blocks
            return 0, jnp.where(i < 2 * blocks, early, tail)

        return pl.BlockSpec((channels, WIDE), at)

    def attend_weight(depth, which):
        at = lambda i: (0, jnp.clip(i - blocks, 0, blocks - 1) + which * blocks)
        return pl.BlockSpec((depth, WIDE), at)

    return pl.pallas_call(
        block_kernel,
        grid=(3 * blocks,),
        in_specs=[whole(array) for array in (hidden, values, bias, order, attend_order)]
        + [weight(part) for part in range(3)]
        + [attend_weight(depth, which) for depth in PARTS for which in range(3)],
        out_specs=pl.BlockSpec((count, WIDE), lambda i: (0, jnp.maximum(i - 2 * blocks, 0))),
        out_shape=jax.ShapeDtypeStruct((count, channels), jnp.bfloat16),
        scratch_shapes=[
            pltpu.VMEM((channels, channels), jnp.bfloat16),
            pltpu.VMEM((channels, PADDED), jnp.bfloat16),
            pltpu.VMEM((count, channels), jnp.bfloat16),
            pltpu.VMEM((count, PADDED), jnp.bfloat16),
            pltpu.VMEM((count, channels), jnp.bfloat16),
            pltpu.VMEM((count, channels), jnp.bfloat16),
        ],
        cost_estimate=pl.CostEstimate(
            flops=2 * count * channels * 9 * channels,
            bytes_accessed=14 * channels * channels + 8 * count * channels,
            transcendentals=count * count * HEADS // 2,
        ),
    )(
        hidden, values, bias, order, attend_order, weights, weights, weights,
        *[array for array in attend_weights for _ in range(3)]
    )


def shards(latents, timestep, norm_gain, time_weight, conv_weight, attend_weight, output_weight):
    _, frames_dev, pixels, channels = latents.shape
    my = {axis: lax.axis_index(axis) for axis in ALL}
    frame = my["x"] * 4 + my["y"]

    piece = jnp.concatenate(
        [conv_weight[t] for t in range(3)]
        + [
            output_weight,
            lax.dynamic_index_in_dim(time_weight.reshape(20, 16, 80), frame, 1, False).reshape(5, 320),
        ],
        axis=1,
    ).reshape(-1)
    near = [shifted(piece, "z", step) for step in RING[1:5]]
    flat = attend_weight.reshape(-1)
    line = [flat] + [shifted(flat, "y", step) for step in SMALL[1:]]
    near, line = lax.optimization_barrier((near, line))
    far = [shifted(near[2], "z", 1), shifted(near[3], "z", -1), shifted(near[2], "z", 2)]
    line = jnp.concatenate(line)
    plane = [line] + [shifted(line, "x", step) for step in SMALL[1:]]
    square = jnp.stack(plane).reshape(80, 3 * channels)
    stage = jnp.stack([piece] + near + far).reshape(8, 5, -1)
    mixing = stage[:, :, : 4 * channels].reshape(40, 4 * channels)
    mixing = lax.all_gather(mixing, ("core", "x", "y"), axis=0, tiled=True)

    latents, stage, square = lax.optimization_barrier((latents, stage, square))
    back, ahead = shifted(square, "z", 1), shifted(square, "z", -1)
    chunks = [square, back, ahead]

    here = latents.reshape(-1, channels).astype(jnp.float32)
    width = channels // GROUPS
    members = here.shape[0] * width
    mean_here = jnp.sum(jnp.sum(here, axis=0).reshape(GROUPS, width), axis=1) / members
    deviate = here - jnp.repeat(mean_here, width)[None, :]
    square_here = jnp.sum(jnp.sum(deviate * deviate, axis=0).reshape(GROUPS, width), axis=1)
    features = sinusoid(timestep).astype(jnp.bfloat16).reshape(8, 2, 20)
    features = features[(my["z"] - jnp.asarray(RING)) % 8]
    time_rows = stage[:, :, 4 * channels :].reshape(160, 80)
    time_other = shifted(time_rows, "core", 1)
    bias_here = jnp.zeros((1, 80), jnp.float32)
    for core, rows in ((my["core"], time_rows), (1 - my["core"], time_other)):
        part = lax.dynamic_index_in_dim(features, core, 1, False).reshape(1, 160)
        bias_here = bias_here + jnp.dot(part, rows, preferred_element_type=jnp.float32)
    sums = jnp.concatenate([mean_here, square_here, bias_here[0]])[None, :]
    back, ahead, sums = lax.optimization_barrier((back, ahead, sums))

    back, ahead = shifted(back, "z", 1), shifted(ahead, "z", -1)
    chunks += [back, ahead]
    sums = lax.all_to_all(jnp.broadcast_to(sums[None], (16, *sums.shape)), FRAME, 0, 0, tiled=True)
    back, ahead, sums = lax.optimization_barrier((back, ahead, sums))

    back, ahead = shifted(back, "z", 1), shifted(ahead, "z", -1)
    chunks += [back, ahead]
    latents, _ = lax.optimization_barrier((latents, sums))
    values = lax.all_to_all(latents, FRAME, split_axis=2, concat_axis=1, tiled=True)
    back, values = lax.optimization_barrier((back, values))
    chunks.append(shifted(back, "z", 1))
    values = values.reshape(-1, channels)
    sums = sums.reshape(16, -1)
    means, squares = sums[:, :GROUPS], sums[:, GROUPS : 2 * GROUPS]
    time_bias = sums[:, 2 * GROUPS :].reshape(1, channels)
    center = jnp.mean(means, axis=0)
    spread = jnp.sum(squares, axis=0) + members * jnp.sum((means - center) ** 2, axis=0)
    spread = spread / (16 * members)
    scale = norm_gain / jnp.sqrt(jnp.repeat(spread, width) + 1e-05)

    ring, small = np.array(RING), np.array(SMALL)
    core, x, y, z, row = np.indices((2, 4, 4, 8, 5)).reshape(5, -1)
    order = channel_of((my["z"] - ring[z]) % 8, core, x, y, row)
    part, z, x, y, row = np.indices((2, 8, 4, 4, 5)).reshape(5, -1)
    core = jnp.where(part == 0, my["core"], 1 - my["core"])
    places = [(my["z"] - ring[z]) % 8, core, (my["x"] - small[x]) % 4, (my["y"] - small[y]) % 4]
    attend_order = channel_of(*places, row)

    center = jnp.repeat(center, width)[None, :]
    hidden = hidden_of(values, center, scale[None, :], order[None, :])
    own = jnp.concatenate(chunks, axis=0)
    own, mixing, hidden, time_bias, order, attend_order = lax.optimization_barrier(
        (own, mixing, hidden, time_bias, order[None, :], attend_order[None, :])
    )
    attending = [own, shifted(own, "core", 1)]
    residual, mixed = convolve(hidden, values, time_bias, attend_order, mixing)
    mixed = attend(mixed, residual, order, attending, mixing)
    mixed = mixed.reshape(1, -1, 8, channels)
    return lax.all_to_all(mixed, FRAME, split_axis=1, concat_axis=2, tiled=True)


def solution(mesh):
    split = Mesh(mesh.devices.reshape(8, 2, 4, 4), ALL)
    placed = (
        P(DP, FRAME, None, None),
        P(DP),
        P(),
        P(DP, None),
        P(None, ALL, None),
        P(ALL, None),
        P(ALL, None),
    )
    return jax.shard_map(
        shards, mesh=split, in_specs=placed, out_specs=P(DP, FRAME, None, None), check_vma=False
    )
```

```python
import math

import jax
import jax.numpy as jnp
import numpy as np
from jax import lax
from jax.experimental import pallas as pl
from jax.experimental.pallas import tpu as pltpu
from jax.sharding import Mesh
from jax.sharding import PartitionSpec as P


HEADS = 20
HD = 64
GROUPS = 32
TEMB = 320
FRAME = ("x", "y")
DP = ("z", "core")
ALL = ("z", "core", "x", "y")


def shifted(array, axis, step):
    count = lax.axis_size(axis)
    return lax.ppermute(array, axis, [(i, (i + step) % count) for i in range(count)])


RING = (0, 1, -1, 2, -2, 3, -3, 4)
SMALL = (0, 1, -1, 2)


def channel_of(z, core, x, y, row):
    return z * 160 + core * 80 + x * 20 + y * 5 + row


def moved(array, table):
    return jnp.dot(array, table, preferred_element_type=jnp.float32).astype(jnp.bfloat16)


def sinusoid(timestep):
    half_dim = TEMB // 2
    ladder = jnp.arange(half_dim, dtype=jnp.float32)
    freqs = jnp.exp(-math.log(10000.0) * ladder / half_dim)
    angles = timestep.astype(jnp.float32)[:, None] * freqs[None, :]
    return jnp.concatenate([jnp.cos(angles), jnp.sin(angles)], axis=-1)


def attended_pair(query, key, value, first, same):
    results = []
    for mine in (first, jnp.logical_not(first)):
        part = jnp.where(mine, query, jnp.zeros_like(query)) * (1.0 / math.sqrt(HD))
        scores = lax.dot_general(
            part.astype(jnp.bfloat16),
            key,
            (((1,), (1,)), ((), ())),
            preferred_element_type=jnp.float32,
        )
        scores = jnp.where(same, scores, -3e38)
        expo = jnp.exp(scores - jnp.max(scores, axis=-1, keepdims=True)).astype(jnp.bfloat16)
        padded = jnp.where(mine, value, jnp.ones_like(value))
        results.append(jnp.dot(expo, padded, preferred_element_type=jnp.float32))
    sums = pltpu.roll(jnp.where(first, results[1], results[0]), HD, 1)
    return (jnp.where(first, results[0], results[1]) / sums).astype(jnp.bfloat16)


WIDE = 256
PADDED = 1280
PARTS = (640, 640)


def fill(table_ref, order_ref, lanes):
    order = order_ref[:, lanes]
    channel = lax.broadcasted_iota(jnp.int32, (table_ref.shape[0], order.shape[1]), 0)
    table_ref[:, lanes] = (channel == order).astype(jnp.bfloat16)


def conv_kernel(
    hidden_ref, values_ref, bias_ref, order_ref, first_ref, middle_ref, last_ref,
    residual_ref, mixed_ref, table_ref, held_ref
):
    count, channels = hidden_ref.shape
    frames = count // 8
    blocks = channels // WIDE
    step = pl.program_id(0)
    @pl.when(step < blocks)
    def _():
        lanes = pl.ds(pl.multiple_of(step * WIDE, WIDE), WIDE)
        fill(table_ref, order_ref, lanes)
        hidden = hidden_ref[...]
        first, middle, last = [
            jnp.dot(hidden, ref[...], preferred_element_type=jnp.float32)
            for ref in (first_ref, middle_ref, last_ref)
        ]
        edge = jnp.zeros((8, WIDE), jnp.float32)
        before = jnp.concatenate([edge, first[:-8]], axis=0)
        after = jnp.concatenate([last[8:], edge], axis=0)
        conv = before + middle + after + bias_ref[:, lanes]
        residual_ref[:, lanes] = (values_ref[:, lanes].astype(jnp.float32) + conv).astype(
            jnp.bfloat16
        )

    @pl.when(step == blocks)
    def _():
        to = lax.broadcasted_iota(jnp.int32, (count, count), 0)
        source = lax.broadcasted_iota(jnp.int32, (count, count), 1)
        rows = residual_ref[...].astype(jnp.float32)
        centered = rows - jnp.mean(rows, axis=-1, keepdims=True)
        variance = jnp.mean(centered * centered, axis=-1, keepdims=True)
        normed = (centered / jnp.sqrt(variance + 1e-05)).astype(jnp.bfloat16)
        by_pixel = (source == (to % frames) * 8 + to // frames).astype(jnp.bfloat16)
        held_ref[...] = moved(by_pixel, normed)

        @pl.loop(0, PADDED // WIDE)
        def _(part):
            lanes = pl.ds(pl.multiple_of(part * WIDE, WIDE), WIDE)
            mixed_ref[:, lanes] = moved(held_ref[...], table_ref[:, lanes])


def convolve(hidden, values, bias, order, weights):
    count, channels = hidden.shape
    blocks = channels // WIDE
    whole = lambda array: pl.BlockSpec(array.shape, lambda i: (0, 0))
    weight = lambda tap: pl.BlockSpec(
        (channels, WIDE), lambda i: (0, jnp.minimum(i, blocks - 1) + tap * blocks)
    )
    shapes = [jax.ShapeDtypeStruct((count, w), jnp.bfloat16) for w in (channels, PADDED)]
    return pl.pallas_call(
        conv_kernel,
        grid=(blocks + 1,),
        in_specs=[whole(array) for array in (hidden, values, bias, order)]
        + [weight(tap) for tap in range(3)],
        out_specs=[whole(shape) for shape in shapes],
        out_shape=shapes,
        scratch_shapes=[
            pltpu.VMEM((channels, PADDED), jnp.bfloat16),
            pltpu.VMEM((count, channels), jnp.bfloat16),
        ],
        cost_estimate=pl.CostEstimate(
            flops=2 * count * channels * 4 * channels,
            bytes_accessed=6 * channels * channels + 10 * count * channels,
            transcendentals=0,
        ),
    )(hidden, values, bias, order, weights, weights, weights)


def attend_kernel(mixed_ref, residual_ref, order_ref, *refs):
    attend_refs, refs = refs[: 3 * len(PARTS)], refs[3 * len(PARTS) :]
    output_ref, out_ref, triple_ref, table_ref, held_ref, attended_ref = refs
    count, channels = residual_ref.shape
    frames = count // 8
    blocks = channels // WIDE
    step = pl.program_id(0)
    product = lambda left, right: jnp.dot(left, right, preferred_element_type=jnp.float32)

    @pl.when(step <= blocks)
    def _():
        now, before = step % 2, (step + 1) % 2
        query, key, value = [triple_ref[before, which] for which in range(3)]
        for which in range(3):
            weight = [attend_refs[part * 3 + which][...] for part in range(len(PARTS))]
            weight = jnp.concatenate(weight, axis=0)
            triple_ref[now, which] = product(mixed_ref[...], weight).astype(jnp.bfloat16)
        group = count // 2
        first = lax.broadcasted_iota(jnp.int32, (group, 128), 1) < HD
        same = (
            lax.broadcasted_iota(jnp.int32, (group, group), 0) // frames
            == lax.broadcasted_iota(jnp.int32, (group, group), 1) // frames
        )
        base = jnp.maximum(step - 1, 0) * WIDE
        for place in range(2):
            cut = slice(place * group, (place + 1) * group)
            for pair in range(WIDE // 128):
                lanes = slice(pair * 128, (pair + 1) * 128)
                target = pl.ds(pl.multiple_of(base + pair * 128, 128), 128)
                attended_ref[cut, target] = attended_pair(
                    query[cut, lanes], key[cut, lanes], value[cut, lanes], first, same
                )
        fill(table_ref, order_ref, pl.ds(pl.multiple_of(base, WIDE), WIDE))

    @pl.when(step == blocks + 1)
    def _():
        to = lax.broadcasted_iota(jnp.int32, (count, count), 0)
        source = lax.broadcasted_iota(jnp.int32, (count, count), 1)
        by_frame = (source == (to % 8) * frames + to // 8).astype(jnp.bfloat16)
        attended_ref[...] = moved(by_frame, attended_ref[...])

        @pl.loop(0, blocks)
        def _(part):
            lanes = pl.ds(pl.multiple_of(part * WIDE, WIDE), WIDE)
            held_ref[:, lanes] = moved(attended_ref[...], table_ref[:, lanes])

    @pl.when(step > blocks)
    def _():
        lanes = pl.ds(pl.multiple_of((step - blocks - 1) * WIDE, WIDE), WIDE)
        rows = residual_ref[:, lanes].astype(jnp.float32)
        out_ref[...] = (rows + product(held_ref[...], output_ref[...])).astype(jnp.bfloat16)


def attend(mixed, residual, order, attend_weights, weights):
    count, channels = residual.shape
    blocks = channels // WIDE
    whole = lambda array: pl.BlockSpec(array.shape, lambda i: (0, 0))
    late = lambda i: jnp.maximum(i - blocks - 1, 0)

    def attend_weight(depth, which):
        at = lambda i: (0, jnp.minimum(i, blocks - 1) + which * blocks)
        return pl.BlockSpec((depth, WIDE), at)

    return pl.pallas_call(
        attend_kernel,
        grid=(2 * blocks + 1,),
        in_specs=[whole(array) for array in (mixed, residual, order)]
        + [attend_weight(depth, which) for depth in PARTS for which in range(3)]
        + [pl.BlockSpec((channels, WIDE), lambda i: (0, late(i) + 3 * blocks))],
        out_specs=pl.BlockSpec((count, WIDE), lambda i: (0, late(i))),
        out_shape=jax.ShapeDtypeStruct((count, channels), jnp.bfloat16),
        scratch_shapes=[
            pltpu.VMEM((2, 3, count, WIDE), jnp.bfloat16),
            pltpu.VMEM((channels, channels), jnp.bfloat16),
            pltpu.VMEM((count, channels), jnp.bfloat16),
            pltpu.VMEM((count, channels), jnp.bfloat16),
        ],
        cost_estimate=pl.CostEstimate(
            flops=2 * count * channels * 5 * channels,
            bytes_accessed=8 * channels * channels + 8 * count * channels,
            transcendentals=count * count * HEADS // 2,
        ),
    )(mixed, residual, order, *[a for a in attend_weights for _ in range(3)], weights)


def hidden_kernel(values_ref, center_ref, scale_ref, order_ref, out_ref, held_ref, table_ref):
    scaled = (values_ref[...].astype(jnp.float32) - center_ref[...]) * scale_ref[...]
    held_ref[...] = jax.nn.silu(scaled).astype(jnp.bfloat16)

    @pl.loop(0, held_ref.shape[1] // WIDE)
    def _(part):
        lanes = pl.ds(pl.multiple_of(part * WIDE, WIDE), WIDE)
        order = order_ref[:, lanes]
        channel = lax.broadcasted_iota(jnp.int32, table_ref.shape, 0)
        table_ref[...] = (channel == order).astype(jnp.bfloat16)
        out_ref[:, lanes] = moved(held_ref[...], table_ref[...])


def hidden_of(values, center, scale, order):
    return pl.pallas_call(
        hidden_kernel,
        out_shape=jax.ShapeDtypeStruct(values.shape, jnp.bfloat16),
        scratch_shapes=[
            pltpu.VMEM(values.shape, jnp.bfloat16),
            pltpu.VMEM((values.shape[1], WIDE), jnp.bfloat16),
        ],
        cost_estimate=pl.CostEstimate(
            flops=2 * values.shape[0] * values.shape[1] ** 2,
            bytes_accessed=4 * values.size,
            transcendentals=values.size,
        ),
    )(values, center, scale, order)


def block(hidden, values, bias, order, attend_order, weights, attend_weights):
    count, channels = hidden.shape
    blocks = channels // WIDE
    whole = lambda array: pl.BlockSpec(array.shape, lambda i: (0, 0))

    def weight(part):
        def at(i):
            tail = i + blocks if part == 0 else part * blocks + blocks - 1
            early = jnp.minimum(i, blocks - 1) + part * blocks
            return 0, jnp.where(i < 2 * blocks, early, tail)

        return pl.BlockSpec((channels, WIDE), at)

    def attend_weight(depth, which):
        at = lambda i: (0, jnp.clip(i - blocks, 0, blocks - 1) + which * blocks)
        return pl.BlockSpec((depth, WIDE), at)

    return pl.pallas_call(
        block_kernel,
        grid=(3 * blocks,),
        in_specs=[whole(array) for array in (hidden, values, bias, order, attend_order)]
        + [weight(part) for part in range(3)]
        + [attend_weight(depth, which) for depth in PARTS for which in range(3)],
        out_specs=pl.BlockSpec((count, WIDE), lambda i: (0, jnp.maximum(i - 2 * blocks, 0))),
        out_shape=jax.ShapeDtypeStruct((count, channels), jnp.bfloat16),
        scratch_shapes=[
            pltpu.VMEM((channels, channels), jnp.bfloat16),
            pltpu.VMEM((channels, PADDED), jnp.bfloat16),
            pltpu.VMEM((count, channels), jnp.bfloat16),
            pltpu.VMEM((count, PADDED), jnp.bfloat16),
            pltpu.VMEM((count, channels), jnp.bfloat16),
            pltpu.VMEM((count, channels), jnp.bfloat16),
        ],
        cost_estimate=pl.CostEstimate(
            flops=2 * count * channels * 9 * channels,
            bytes_accessed=14 * channels * channels + 8 * count * channels,
            transcendentals=count * count * HEADS // 2,
        ),
    )(
        hidden, values, bias, order, attend_order, weights, weights, weights,
        *[array for array in attend_weights for _ in range(3)]
    )


def shards(latents, timestep, norm_gain, time_weight, conv_weight, attend_weight, output_weight):
    _, frames_dev, pixels, channels = latents.shape
    my = {axis: lax.axis_index(axis) for axis in ALL}
    frame = my["x"] * 4 + my["y"]

    piece = jnp.concatenate(
        [conv_weight[t] for t in range(3)]
        + [
            output_weight,
            lax.dynamic_index_in_dim(time_weight.reshape(20, 16, 80), frame, 1, False).reshape(5, 320),
        ],
        axis=1,
    ).reshape(-1)
    near = [shifted(piece, "z", step) for step in RING[1:5]]
    flat = attend_weight.reshape(-1)
    line = [flat] + [shifted(flat, "y", step) for step in SMALL[1:]]
    near, line = lax.optimization_barrier((near, line))
    far = [shifted(near[2], "z", 1), shifted(near[3], "z", -1), shifted(near[2], "z", 2)]
    line = jnp.concatenate(line)
    plane = [line] + [shifted(line, "x", step) for step in SMALL[1:]]
    square = jnp.stack(plane).reshape(80, 3 * channels)
    stage = jnp.stack([piece] + near + far).reshape(8, 5, -1)
    mixing = stage[:, :, : 4 * channels].reshape(40, 4 * channels)
    mixing = lax.all_gather(mixing, ("core", "x", "y"), axis=0, tiled=True)

    latents, stage, square = lax.optimization_barrier((latents, stage, square))
    back, ahead = shifted(square, "z", 1), shifted(square, "z", -1)
    chunks = [square, back, ahead]

    values = lax.all_to_all(latents, FRAME, split_axis=2, concat_axis=1, tiled=True)

    here = latents.reshape(-1, channels).astype(jnp.float32)
    width = channels // GROUPS
    members = here.shape[0] * width
    mean_here = jnp.sum(jnp.sum(here, axis=0).reshape(GROUPS, width), axis=1) / members
    deviate = here - jnp.repeat(mean_here, width)[None, :]
    square_here = jnp.sum(jnp.sum(deviate * deviate, axis=0).reshape(GROUPS, width), axis=1)
    features = sinusoid(timestep).astype(jnp.bfloat16).reshape(8, 2, 20)
    features = features[(my["z"] - jnp.asarray(RING)) % 8]
    time_rows = stage[:, :, 4 * channels :].reshape(160, 80)
    time_other = shifted(time_rows, "core", 1)
    bias_here = jnp.zeros((1, 80), jnp.float32)
    for core, rows in ((my["core"], time_rows), (1 - my["core"], time_other)):
        part = lax.dynamic_index_in_dim(features, core, 1, False).reshape(1, 160)
        bias_here = bias_here + jnp.dot(part, rows, preferred_element_type=jnp.float32)
    sums = jnp.concatenate([mean_here, square_here, bias_here[0]])[None, :]
    back, ahead, sums, values = lax.optimization_barrier((back, ahead, sums, values))
    values = values.reshape(-1, channels)

    back, ahead = shifted(back, "z", 1), shifted(ahead, "z", -1)
    chunks += [back, ahead]
    sums = lax.all_to_all(jnp.broadcast_to(sums[None], (16, *sums.shape)), FRAME, 0, 0, tiled=True)
    back, ahead, sums = lax.optimization_barrier((back, ahead, sums))

    back, ahead = shifted(back, "z", 1), shifted(ahead, "z", -1)
    chunks += [back, ahead]
    chunks.append(shifted(back, "z", 1))
    sums = sums.reshape(16, -1)
    means, squares = sums[:, :GROUPS], sums[:, GROUPS : 2 * GROUPS]
    time_bias = sums[:, 2 * GROUPS :].reshape(1, channels)
    center = jnp.mean(means, axis=0)
    spread = jnp.sum(squares, axis=0) + members * jnp.sum((means - center) ** 2, axis=0)
    spread = spread / (16 * members)
    scale = norm_gain / jnp.sqrt(jnp.repeat(spread, width) + 1e-05)

    ring, small = np.array(RING), np.array(SMALL)
    core, x, y, z, row = np.indices((2, 4, 4, 8, 5)).reshape(5, -1)
    order = channel_of((my["z"] - ring[z]) % 8, core, x, y, row)
    part, z, x, y, row = np.indices((2, 8, 4, 4, 5)).reshape(5, -1)
    core = jnp.where(part == 0, my["core"], 1 - my["core"])
    places = [(my["z"] - ring[z]) % 8, core, (my["x"] - small[x]) % 4, (my["y"] - small[y]) % 4]
    attend_order = channel_of(*places, row)

    center = jnp.repeat(center, width)[None, :]
    hidden = hidden_of(values, center, scale[None, :], order[None, :])
    own = jnp.concatenate(chunks, axis=0)
    own, mixing, hidden, time_bias, order, attend_order = lax.optimization_barrier(
        (own, mixing, hidden, time_bias, order[None, :], attend_order[None, :])
    )
    attending = [own, shifted(own, "core", 1)]
    residual, mixed = convolve(hidden, values, time_bias, attend_order, mixing)
    mixed = attend(mixed, residual, order, attending, mixing)
    mixed = mixed.reshape(1, -1, 8, channels)
    return lax.all_to_all(mixed, FRAME, split_axis=1, concat_axis=2, tiled=True)


def solution(mesh):
    split = Mesh(mesh.devices.reshape(8, 2, 4, 4), ALL)
    placed = (
        P(DP, FRAME, None, None),
        P(DP),
        P(),
        P(DP, None),
        P(None, ALL, None),
        P(ALL, None),
        P(ALL, None),
    )
    return jax.shard_map(
        shards, mesh=split, in_specs=placed, out_specs=P(DP, FRAME, None, None), check_vma=False
    )
```

```python
import math

import jax
import jax.numpy as jnp
import numpy as np
from jax import lax
from jax.experimental import pallas as pl
from jax.experimental.pallas import tpu as pltpu
from jax.sharding import Mesh
from jax.sharding import PartitionSpec as P


HEADS = 20
HD = 64
GROUPS = 32
TEMB = 320
FRAME = ("x", "y")
DP = ("z", "core")
ALL = ("z", "core", "x", "y")


def shifted(array, axis, step):
    count = lax.axis_size(axis)
    return lax.ppermute(array, axis, [(i, (i + step) % count) for i in range(count)])


RING = (0, 1, -1, 2, -2, 3, -3, 4)
SMALL = (0, 1, -1, 2)


def channel_of(z, core, x, y, row):
    return z * 160 + core * 80 + x * 20 + y * 5 + row


def moved(array, table):
    return jnp.dot(array, table, preferred_element_type=jnp.float32).astype(jnp.bfloat16)


def sinusoid(timestep):
    half_dim = TEMB // 2
    ladder = jnp.arange(half_dim, dtype=jnp.float32)
    freqs = jnp.exp(-math.log(10000.0) * ladder / half_dim)
    angles = timestep.astype(jnp.float32)[:, None] * freqs[None, :]
    return jnp.concatenate([jnp.cos(angles), jnp.sin(angles)], axis=-1)


def attended_pair(query, key, value, first, same):
    results = []
    for mine in (first, jnp.logical_not(first)):
        part = jnp.where(mine, query, jnp.zeros_like(query)) * (1.0 / math.sqrt(HD))
        scores = lax.dot_general(
            part.astype(jnp.bfloat16),
            key,
            (((1,), (1,)), ((), ())),
            preferred_element_type=jnp.float32,
        )
        scores = jnp.where(same, scores, -3e38)
        expo = jnp.exp(scores - jnp.max(scores, axis=-1, keepdims=True)).astype(jnp.bfloat16)
        padded = jnp.where(mine, value, jnp.ones_like(value))
        results.append(jnp.dot(expo, padded, preferred_element_type=jnp.float32))
    sums = pltpu.roll(jnp.where(first, results[1], results[0]), HD, 1)
    return (jnp.where(first, results[0], results[1]) / sums).astype(jnp.bfloat16)


WIDE = 256
PADDED = 1280
PARTS = (640, 640)


def fill(table_ref, order_ref, lanes):
    order = order_ref[:, lanes]
    channel = lax.broadcasted_iota(jnp.int32, (table_ref.shape[0], order.shape[1]), 0)
    table_ref[:, lanes] = (channel == order).astype(jnp.bfloat16)


def conv_kernel(
    hidden_ref, values_ref, bias_ref, order_ref, first_ref, middle_ref, last_ref,
    residual_ref, mixed_ref, table_ref, held_ref
):
    count, channels = hidden_ref.shape
    frames = count // 8
    blocks = channels // WIDE
    step = pl.program_id(0)
    @pl.when(step < blocks)
    def _():
        lanes = pl.ds(pl.multiple_of(step * WIDE, WIDE), WIDE)
        fill(table_ref, order_ref, lanes)
        hidden = hidden_ref[...]
        first, middle, last = [
            jnp.dot(hidden, ref[...], preferred_element_type=jnp.float32)
            for ref in (first_ref, middle_ref, last_ref)
        ]
        edge = jnp.zeros((8, WIDE), jnp.float32)
        before = jnp.concatenate([edge, first[:-8]], axis=0)
        after = jnp.concatenate([last[8:], edge], axis=0)
        conv = before + middle + after + bias_ref[:, lanes]
        residual_ref[:, lanes] = (values_ref[:, lanes].astype(jnp.float32) + conv).astype(
            jnp.bfloat16
        )

    @pl.when(step == blocks)
    def _():
        to = lax.broadcasted_iota(jnp.int32, (count, count), 0)
        source = lax.broadcasted_iota(jnp.int32, (count, count), 1)
        rows = residual_ref[...].astype(jnp.float32)
        centered = rows - jnp.mean(rows, axis=-1, keepdims=True)
        variance = jnp.mean(centered * centered, axis=-1, keepdims=True)
        normed = (centered / jnp.sqrt(variance + 1e-05)).astype(jnp.bfloat16)
        by_pixel = (source == (to % frames) * 8 + to // frames).astype(jnp.bfloat16)
        held_ref[...] = moved(by_pixel, normed)

        @pl.loop(0, PADDED // WIDE)
        def _(part):
            lanes = pl.ds(pl.multiple_of(part * WIDE, WIDE), WIDE)
            mixed_ref[:, lanes] = moved(held_ref[...], table_ref[:, lanes])


def convolve(hidden, values, bias, order, weights):
    count, channels = hidden.shape
    blocks = channels // WIDE
    whole = lambda array: pl.BlockSpec(array.shape, lambda i: (0, 0))
    weight = lambda tap: pl.BlockSpec(
        (channels, WIDE), lambda i: (0, jnp.minimum(i, blocks - 1) + tap * blocks)
    )
    shapes = [jax.ShapeDtypeStruct((count, w), jnp.bfloat16) for w in (channels, PADDED)]
    return pl.pallas_call(
        conv_kernel,
        grid=(blocks + 1,),
        in_specs=[whole(array) for array in (hidden, values, bias, order)]
        + [weight(tap) for tap in range(3)],
        out_specs=[whole(shape) for shape in shapes],
        out_shape=shapes,
        scratch_shapes=[
            pltpu.VMEM((channels, PADDED), jnp.bfloat16),
            pltpu.VMEM((count, channels), jnp.bfloat16),
        ],
        cost_estimate=pl.CostEstimate(
            flops=2 * count * channels * 4 * channels,
            bytes_accessed=6 * channels * channels + 10 * count * channels,
            transcendentals=0,
        ),
    )(hidden, values, bias, order, weights, weights, weights)


def attend_kernel(mixed_ref, residual_ref, order_ref, *refs):
    attend_refs, refs = refs[: 3 * len(PARTS)], refs[3 * len(PARTS) :]
    output_ref, out_ref, table_ref, held_ref, attended_ref = refs
    count, channels = residual_ref.shape
    frames = count // 8
    blocks = channels // WIDE
    step = pl.program_id(0)
    product = lambda left, right: jnp.dot(left, right, preferred_element_type=jnp.float32)

    @pl.when(step < blocks)
    def _():
        triple = []
        for which in range(3):
            weight = [attend_refs[part * 3 + which][...] for part in range(len(PARTS))]
            weight = jnp.concatenate(weight, axis=0)
            triple.append(product(mixed_ref[...], weight).astype(jnp.bfloat16))
        query, key, value = triple
        group = count // 2
        first = lax.broadcasted_iota(jnp.int32, (group, 128), 1) < HD
        same = (
            lax.broadcasted_iota(jnp.int32, (group, group), 0) // frames
            == lax.broadcasted_iota(jnp.int32, (group, group), 1) // frames
        )
        base = step * WIDE
        for place in range(2):
            cut = slice(place * group, (place + 1) * group)
            for pair in range(WIDE // 128):
                lanes = slice(pair * 128, (pair + 1) * 128)
                target = pl.ds(pl.multiple_of(base + pair * 128, 128), 128)
                attended_ref[cut, target] = attended_pair(
                    query[cut, lanes], key[cut, lanes], value[cut, lanes], first, same
                )
        fill(table_ref, order_ref, pl.ds(pl.multiple_of(base, WIDE), WIDE))

    @pl.when(step == blocks)
    def _():
        to = lax.broadcasted_iota(jnp.int32, (count, count), 0)
        source = lax.broadcasted_iota(jnp.int32, (count, count), 1)
        by_frame = (source == (to % 8) * frames + to // 8).astype(jnp.bfloat16)
        attended_ref[...] = moved(by_frame, attended_ref[...])

        @pl.loop(0, blocks)
        def _(part):
            lanes = pl.ds(pl.multiple_of(part * WIDE, WIDE), WIDE)
            held_ref[:, lanes] = moved(attended_ref[...], table_ref[:, lanes])

    @pl.when(step >= blocks)
    def _():
        lanes = pl.ds(pl.multiple_of((step - blocks) * WIDE, WIDE), WIDE)
        rows = residual_ref[:, lanes].astype(jnp.float32)
        out_ref[...] = (rows + product(held_ref[...], output_ref[...])).astype(jnp.bfloat16)


def attend(mixed, residual, order, attend_weights, weights):
    count, channels = residual.shape
    blocks = channels // WIDE
    whole = lambda array: pl.BlockSpec(array.shape, lambda i: (0, 0))
    late = lambda i: jnp.maximum(i - blocks, 0)

    def attend_weight(depth, which):
        at = lambda i: (0, jnp.minimum(i, blocks - 1) + which * blocks)
        return pl.BlockSpec((depth, WIDE), at)

    return pl.pallas_call(
        attend_kernel,
        grid=(2 * blocks,),
        in_specs=[whole(array) for array in (mixed, residual, order)]
        + [attend_weight(depth, which) for depth in PARTS for which in range(3)]
        + [pl.BlockSpec((channels, WIDE), lambda i: (0, late(i) + 3 * blocks))],
        out_specs=pl.BlockSpec((count, WIDE), lambda i: (0, late(i))),
        out_shape=jax.ShapeDtypeStruct((count, channels), jnp.bfloat16),
        scratch_shapes=[
            pltpu.VMEM((channels, channels), jnp.bfloat16),
            pltpu.VMEM((count, channels), jnp.bfloat16),
            pltpu.VMEM((count, channels), jnp.bfloat16),
        ],
        cost_estimate=pl.CostEstimate(
            flops=2 * count * channels * 5 * channels,
            bytes_accessed=8 * channels * channels + 8 * count * channels,
            transcendentals=count * count * HEADS // 2,
        ),
    )(mixed, residual, order, *[a for a in attend_weights for _ in range(3)], weights)


def hidden_kernel(values_ref, center_ref, scale_ref, order_ref, out_ref, held_ref, table_ref):
    scaled = (values_ref[...].astype(jnp.float32) - center_ref[...]) * scale_ref[...]
    held_ref[...] = jax.nn.silu(scaled).astype(jnp.bfloat16)

    @pl.loop(0, held_ref.shape[1] // WIDE)
    def _(part):
        lanes = pl.ds(pl.multiple_of(part * WIDE, WIDE), WIDE)
        order = order_ref[:, lanes]
        channel = lax.broadcasted_iota(jnp.int32, table_ref.shape, 0)
        table_ref[...] = (channel == order).astype(jnp.bfloat16)
        out_ref[:, lanes] = moved(held_ref[...], table_ref[...])


def hidden_of(values, center, scale, order):
    return pl.pallas_call(
        hidden_kernel,
        out_shape=jax.ShapeDtypeStruct(values.shape, jnp.bfloat16),
        scratch_shapes=[
            pltpu.VMEM(values.shape, jnp.bfloat16),
            pltpu.VMEM((values.shape[1], WIDE), jnp.bfloat16),
        ],
        cost_estimate=pl.CostEstimate(
            flops=2 * values.shape[0] * values.shape[1] ** 2,
            bytes_accessed=4 * values.size,
            transcendentals=values.size,
        ),
    )(values, center, scale, order)


def block(hidden, values, bias, order, attend_order, weights, attend_weights):
    count, channels = hidden.shape
    blocks = channels // WIDE
    whole = lambda array: pl.BlockSpec(array.shape, lambda i: (0, 0))

    def weight(part):
        def at(i):
            tail = i + blocks if part == 0 else part * blocks + blocks - 1
            early = jnp.minimum(i, blocks - 1) + part * blocks
            return 0, jnp.where(i < 2 * blocks, early, tail)

        return pl.BlockSpec((channels, WIDE), at)

    def attend_weight(depth, which):
        at = lambda i: (0, jnp.clip(i - blocks, 0, blocks - 1) + which * blocks)
        return pl.BlockSpec((depth, WIDE), at)

    return pl.pallas_call(
        block_kernel,
        grid=(3 * blocks,),
        in_specs=[whole(array) for array in (hidden, values, bias, order, attend_order)]
        + [weight(part) for part in range(3)]
        + [attend_weight(depth, which) for depth in PARTS for which in range(3)],
        out_specs=pl.BlockSpec((count, WIDE), lambda i: (0, jnp.maximum(i - 2 * blocks, 0))),
        out_shape=jax.ShapeDtypeStruct((count, channels), jnp.bfloat16),
        scratch_shapes=[
            pltpu.VMEM((channels, channels), jnp.bfloat16),
            pltpu.VMEM((channels, PADDED), jnp.bfloat16),
            pltpu.VMEM((count, channels), jnp.bfloat16),
            pltpu.VMEM((count, PADDED), jnp.bfloat16),
            pltpu.VMEM((count, channels), jnp.bfloat16),
            pltpu.VMEM((count, channels), jnp.bfloat16),
        ],
        cost_estimate=pl.CostEstimate(
            flops=2 * count * channels * 9 * channels,
            bytes_accessed=14 * channels * channels + 8 * count * channels,
            transcendentals=count * count * HEADS // 2,
        ),
    )(
        hidden, values, bias, order, attend_order, weights, weights, weights,
        *[array for array in attend_weights for _ in range(3)]
    )


def shards(latents, timestep, norm_gain, time_weight, conv_weight, attend_weight, output_weight):
    _, frames_dev, pixels, channels = latents.shape
    my = {axis: lax.axis_index(axis) for axis in ALL}
    frame = my["x"] * 4 + my["y"]

    piece = jnp.concatenate(
        [conv_weight[t] for t in range(3)]
        + [
            output_weight,
            lax.dynamic_index_in_dim(time_weight.reshape(20, 16, 80), frame, 1, False).reshape(5, 320),
        ],
        axis=1,
    ).reshape(-1)
    near = [shifted(piece, "z", step) for step in RING[1:5]]
    flat = attend_weight.reshape(-1)
    line = [flat] + [shifted(flat, "y", step) for step in SMALL[1:]]
    near, line = lax.optimization_barrier((near, line))
    far = [shifted(near[2], "z", 1), shifted(near[3], "z", -1), shifted(near[2], "z", 2)]
    line = jnp.concatenate(line)
    plane = [line] + [shifted(line, "x", step) for step in SMALL[1:]]
    square = jnp.stack(plane).reshape(80, 3 * channels)
    stage = jnp.stack([piece] + near + far).reshape(8, 5, -1)
    mixing = stage[:, :, : 4 * channels].reshape(40, 4 * channels)
    mixing = lax.all_gather(mixing, ("core", "x", "y"), axis=0, tiled=True)

    latents, stage, square = lax.optimization_barrier((latents, stage, square))
    back, ahead = shifted(square, "z", 1), shifted(square, "z", -1)
    chunks = [square, back, ahead]

    here = latents.reshape(-1, channels).astype(jnp.float32)
    width = channels // GROUPS
    members = here.shape[0] * width
    mean_here = jnp.sum(jnp.sum(here, axis=0).reshape(GROUPS, width), axis=1) / members
    deviate = here - jnp.repeat(mean_here, width)[None, :]
    square_here = jnp.sum(jnp.sum(deviate * deviate, axis=0).reshape(GROUPS, width), axis=1)
    features = sinusoid(timestep).astype(jnp.bfloat16).reshape(8, 2, 20)
    features = features[(my["z"] - jnp.asarray(RING)) % 8]
    time_rows = stage[:, :, 4 * channels :].reshape(160, 80)
    time_other = shifted(time_rows, "core", 1)
    bias_here = jnp.zeros((1, 80), jnp.float32)
    for core, rows in ((my["core"], time_rows), (1 - my["core"], time_other)):
        part = lax.dynamic_index_in_dim(features, core, 1, False).reshape(1, 160)
        bias_here = bias_here + jnp.dot(part, rows, preferred_element_type=jnp.float32)
    sums = jnp.concatenate([mean_here, square_here, bias_here[0]])[None, :]
    back, ahead, sums = lax.optimization_barrier((back, ahead, sums))

    back, ahead = shifted(back, "z", 1), shifted(ahead, "z", -1)
    chunks += [back, ahead]
    sums = lax.all_to_all(jnp.broadcast_to(sums[None], (16, *sums.shape)), FRAME, 0, 0, tiled=True)
    back, ahead, sums = lax.optimization_barrier((back, ahead, sums))

    back, ahead = shifted(back, "z", 1), shifted(ahead, "z", -1)
    chunks += [back, ahead]
    latents, _ = lax.optimization_barrier((latents, sums))
    values = lax.all_to_all(latents, FRAME, split_axis=2, concat_axis=1, tiled=True)
    chunks.append(shifted(back, "z", 1))
    values = values.reshape(-1, channels)
    sums = sums.reshape(16, -1)
    means, squares = sums[:, :GROUPS], sums[:, GROUPS : 2 * GROUPS]
    time_bias = sums[:, 2 * GROUPS :].reshape(1, channels)
    center = jnp.mean(means, axis=0)
    spread = jnp.sum(squares, axis=0) + members * jnp.sum((means - center) ** 2, axis=0)
    spread = spread / (16 * members)
    scale = norm_gain / jnp.sqrt(jnp.repeat(spread, width) + 1e-05)

    ring, small = np.array(RING), np.array(SMALL)
    core, x, y, z, row = np.indices((2, 4, 4, 8, 5)).reshape(5, -1)
    order = channel_of((my["z"] - ring[z]) % 8, core, x, y, row)
    part, z, x, y, row = np.indices((2, 8, 4, 4, 5)).reshape(5, -1)
    core = jnp.where(part == 0, my["core"], 1 - my["core"])
    places = [(my["z"] - ring[z]) % 8, core, (my["x"] - small[x]) % 4, (my["y"] - small[y]) % 4]
    attend_order = channel_of(*places, row)

    center = jnp.repeat(center, width)[None, :]
    hidden = hidden_of(values, center, scale[None, :], order[None, :])
    own = jnp.concatenate(chunks, axis=0)
    own, mixing, hidden, time_bias, order, attend_order = lax.optimization_barrier(
        (own, mixing, hidden, time_bias, order[None, :], attend_order[None, :])
    )
    attending = [own, shifted(own, "core", 1)]
    residual, mixed = convolve(hidden, values, time_bias, attend_order, mixing)
    mixed = attend(mixed, residual, order, attending, mixing)
    mixed = mixed.reshape(1, -1, 8, channels)
    return lax.all_to_all(mixed, FRAME, split_axis=1, concat_axis=2, tiled=True)


def solution(mesh):
    split = Mesh(mesh.devices.reshape(8, 2, 4, 4), ALL)
    placed = (
        P(DP, FRAME, None, None),
        P(DP),
        P(),
        P(DP, None),
        P(None, ALL, None),
        P(ALL, None),
        P(ALL, None),
    )
    return jax.shard_map(
        shards, mesh=split, in_specs=placed, out_specs=P(DP, FRAME, None, None), check_vma=False
    )
```
